512 devices in a mesh: row: 64 (over y, z_hi, core), col: 8 (over z_lo, x).
Axes of the slice: x: 4, y: 8, z: 8 (z_hi: 4, z_lo: 2; z = z_hi * 2 + z_lo), core: 2. Of those that a mesh axis runs over, the one named last changes fastest.
Arguments:
- grad_x: float32 [6144, 4096], P('row', 'col'), may hold values from -6 to 6
- grad_y: float32 [6144, 4096], P('row', 'col'), may hold values from -6 to 6
- weight_x: float32 [6144, 4096], P('row', 'col'), may hold values from 0.1 to 10
- weight_y: float32 [6144, 4096], P('row', 'col'), may hold values from 0.1 to 10
- anchor: float32 [6144, 4096], P('row', 'col'), may hold values from 0.02 to 0.5
- prior: float32 [6144, 4096], P('row', 'col'), may hold values from -6 to 6
Outputs:
- heights: float32 [6144, 4096], P('row', 'col')
- residual: float32 [6144, 4096], P('row', 'col')
The draws below stay inside these ranges and needn't reach their ends.
All inputs are finite; a program needn't handle non-finite values.
Results may differ from the reference program's by a relative error of at most 0.0002.
Values sent between devices are 32-bit elements; how exact they have to be, the bound alone decides.
A program may use at most 64 MiB of HBM per device.

```python
import math
import jax
import jax.numpy as jnp
from jax import lax

ITERS = 3
SWEEPS = 4
NR = 6144
NC = 4096


def steps_of(stream_key, extent, shards, low, top_value):
    loudness = 1.0
    for position, shards_of in shards:
        draws = jax.random.uniform(jax.random.fold_in(jax.random.fold_in(stream_key, 6), position), (shards_of,), jnp.float32, low / len(shards), top_value / len(shards))
        loudness = loudness * jnp.repeat(jnp.exp(draws), extent[position] // shards_of).reshape((-1,) + (1,) * (len(extent) - 1 - position))
    return loudness


def scatter_about(stream_key, extent, scale, most, split=(), dtype=jnp.bfloat16):
    loudness = steps_of(stream_key, extent, split, -0.22, 0.18) if split else 1.0
    entries = jax.random.normal(stream_key, extent, jnp.float32) * scale * loudness
    return jnp.minimum(jnp.maximum(entries, -most), most).astype(dtype)


def setup_inputs(seed: int = 0) -> dict:
    arg_keys = jax.random.split(jax.random.key(seed), 7)
    grad_x = scatter_about(arg_keys[0], (NR, NC), 1.0, 6.0, ((0, 64), (1, 8)), jnp.float32)
    grad_y = scatter_about(arg_keys[1], (NR, NC), 1.0, 6.0, ((0, 64), (1, 8)), jnp.float32)
    weight_x = jnp.clip(jnp.exp(math.log(10.0) - 4.6051702 * jax.random.uniform(arg_keys[2], (NR, NC), jnp.float32) ** steps_of(arg_keys[2], (NR, NC), ((0, 64), (1, 8)), -0.2, 0.2)), 0.1, 10.0)
    weight_y = jnp.clip(jnp.exp(math.log(10.0) - 4.6051702 * jax.random.uniform(arg_keys[3], (NR, NC), jnp.float32) ** steps_of(arg_keys[3], (NR, NC), ((0, 64), (1, 8)), -0.2, 0.2)), 0.1, 10.0)
    anchor = jnp.clip(jnp.exp(math.log(0.5) - 3.218876 * jax.random.uniform(arg_keys[4], (NR, NC), jnp.float32) ** steps_of(arg_keys[4], (NR, NC), ((0, 64), (1, 8)), -0.2, 0.2)), 0.02, 0.5)
    prior = scatter_about(arg_keys[5], (NR, NC), 1.0, 6.0, ((0, 64), (1, 8)), jnp.float32)
    return dict(grad_x=grad_x, grad_y=grad_y, weight_x=weight_x, weight_y=weight_y, anchor=anchor, prior=prior)


damping = 2.0 / 3.0


def block_view(field):
    return field.reshape(field.shape[0] // 4, 4, field.shape[1] // 4, 4)


def sweep(padded, coarse, coeffs):
    centre = padded[1:-1, 1:-1]
    beside = coeffs[0] * padded[1:-1, :-2] + coeffs[1] * padded[1:-1, 2:]
    beside = beside + coeffs[2] * padded[:-2, 1:-1] + coeffs[3] * padded[2:, 1:-1]
    return (1.0 - damping) * centre + damping * coeffs[4] * (coarse + beside)


def reference(grad_x, grad_y, weight_x, weight_y, anchor, prior):
    total_rows, total_cols = grad_x.shape
    row_ids = lax.broadcasted_iota(jnp.int32, grad_x.shape, 0)
    col_ids = lax.broadcasted_iota(jnp.int32, grad_x.shape, 1)
    right_w = jnp.where(col_ids < total_cols - 1, weight_x, jnp.float32(0.0))
    down_w = jnp.where(row_ids < total_rows - 1, weight_y, jnp.float32(0.0))
    left_w = jnp.pad(right_w, ((0, 0), (1, 0)))[:, :-1]
    up_w = jnp.pad(down_w, ((1, 0), (0, 0)))[:-1, :]
    flux_x = right_w * grad_x
    flux_y = down_w * grad_y
    source = anchor * prior + jnp.pad(flux_x, ((0, 0), (1, 0)))[:, :-1] - flux_x
    source = source + jnp.pad(flux_y, ((1, 0), (0, 0)))[:-1, :] - flux_y
    diag = anchor + left_w + right_w + up_w + down_w
    inverse = 1.0 / diag
    c_left = block_view(left_w)[:, :, :, 0].sum(1)
    c_right = block_view(right_w)[:, :, :, 3].sum(1)
    c_up = block_view(up_w)[:, 0, :, :].sum(2)
    c_down = block_view(down_w)[:, 3, :, :].sum(2)
    c_anchor = block_view(anchor).sum((1, 3))
    c_inverse = 1.0 / (c_anchor + c_left + c_right + c_up + c_down)
    coeffs = (c_left, c_right, c_up, c_down, c_inverse)

    def operate(field):
        padded = jnp.pad(field, 1)
        beside = left_w * padded[1:-1, :-2] + right_w * padded[1:-1, 2:]
        beside = beside + up_w * padded[:-2, 1:-1] + down_w * padded[2:, 1:-1]
        return diag * field - beside

    def precondition(resid):
        coarse = block_view(resid).sum((1, 3))
        level = damping * c_inverse * coarse
        for turn in range(SWEEPS - 1):
            level = sweep(jnp.pad(level, 1), coarse, coeffs)
        spread = jnp.broadcast_to(level[:, None, :, None], (level.shape[0], 4, level.shape[1], 4))
        return inverse * resid + spread.reshape(resid.shape)

    heights = jnp.zeros_like(source)
    residual = source
    smooth = precondition(residual)
    agree = jnp.sum(residual * smooth)
    direction = smooth
    for step in range(ITERS):
        image = operate(direction)
        alpha = agree / jnp.sum(direction * image)
        heights = heights + alpha * direction
        residual = residual - alpha * image
        if step + 1 < ITERS:
            smooth = precondition(residual)
            agree_next = jnp.sum(residual * smooth)
            direction = smooth + (agree_next / agree) * direction
            agree = agree_next
    return heights, residual
```

```python
import functools

import jax
import jax.numpy as jnp
from jax import lax
from jax.experimental import pallas as pl
from jax.experimental.pallas import tpu as pltpu
from jax.sharding import PartitionSpec as P

MESH = pl.DeviceIdType.MESH
F = jnp.float32
OMEGA = 2.0 / 3.0

SPLIT = dict(y=8, zh=4, core=2, zl=2, x=4)


def iota(shape, dim):
    return lax.broadcasted_iota(jnp.int32, shape, dim)


def pick(masks, values):
    out = values[-1]
    for mask, value in zip(masks[:-1][::-1], values[:-1][::-1]):
        out = jnp.where(mask, value, out)
    return out


def lane_gather(x, index):
    return jnp.take_along_axis(x, index, axis=1, mode="promise_in_bounds")


def deal(parts, lane):
    low = [(lane & 3) == q for q in range(4)]
    block = [(lane >> 5) == v for v in range(4)]
    moved = []
    for d in range(4):
        merged = pick([low[(v + d) & 3] for v in range(4)], parts)
        moved.append(lane_gather(merged, 4 * (lane & 31) + (((lane >> 5) + d) & 3)))
    return [pick(block, [moved[(s - v) & 3] for v in range(4)]) for s in range(4)]


def undeal(planes, lane):
    low = [(lane & 3) == q for q in range(4)]
    block = [(lane >> 5) == v for v in range(4)]
    moved = []
    for d in range(4):
        merged = pick(block, [planes[(v + d) & 3] for v in range(4)])
        moved.append(lane_gather(merged, 32 * (((lane & 3) - d) & 3) + (lane >> 2)))
    return [pick(low, [moved[(q - v) & 3] for q in range(4)]) for v in range(4)]


def roll(x, shift, axis):
    shift = shift % x.shape[axis]
    return pltpu.roll(x, shift, axis) if shift else x


def kernel(split, *refs):
    ny, nzh, ncore, nzl, nx = (split[k] for k in ("y", "zh", "core", "zl", "x"))
    nrow, ncol = ny * nzh * ncore, nzl * nx
    inputs, refs = refs[:6], refs[6:]
    heights_ref, resid_ref = refs[:2]
    (raw, rw_ref, dw_ref, diag_ref, inv_ref, lw_ref, uw_ref, r0_ref, u_ref, w_ref,
     s0h, s0v, g0h, g0v, s1h, s1u, s1d, g1h, g1v, sh, su, sd, gh, gv,
     part, slots_a, slots_b, slots_c, done,
     in_sem, out_sem, s0_sem, g0_sem, sx_sem, gx_sem, sr_sem, gr_sem) = refs[2:]

    row, col = lax.axis_index("row"), lax.axis_index("col")
    up, down = lax.rem(row + nrow - 1, nrow), lax.rem(row + 1, nrow)
    left, right = lax.rem(col + ncol - 1, ncol), lax.rem(col + 1, ncol)
    neighbours = [(up, col), (up, left), (up, right), (down, col), (down, left), (down, right), (row, left), (row, right)]

    y, zh, core = row // (nzh * ncore), lax.rem(row // ncore, nzh), lax.rem(row, ncore)
    zl, x = col // nx, lax.rem(col, nx)
    z = zh * nzl + zl

    def device(y, z, core, x):
        return ((y * nzh + z // nzl) * ncore + core, lax.rem(z, nzl) * nx + x)

    na, nb, nc = nx * ncore, ny, nzh * nzl
    me_a = x * ncore + core

    def partner_a(k):
        other = lax.rem(me_a + k, na)
        return device(y, z, lax.rem(other, ncore), other // ncore)

    def partner_b(k):
        return device(lax.rem(y + k, ny), z, core, x)

    def partner_c(k):
        return device(y, lax.rem(z + k, nc), core, x)

    loads = [
        [pltpu.make_async_copy(src.at[:, 128 * v:128 * v + 128], raw.at[k, v], in_sem.at[k, v]) for v in range(4)]
        for k, src in enumerate(inputs)
    ]
    for k in (2, 3, 0, 1, 4, 5):
        for copy in loads[k]:
            copy.start()

    partners = neighbours + [partner_a(k) for k in range(1, na)]
    partners += [partner_b(k) for k in range(1, nb)] + [partner_c(k) for k in range(1, nc)]
    barrier = pltpu.get_barrier_semaphore()
    for who in partners:
        pl.semaphore_signal(barrier, inc=1, device_id=who, device_id_type=MESH)

    shape = (24, 128)
    lane, sub = iota(shape, 1), iota(shape, 0)
    lane8, sub8 = iota((8, 128), 1), iota((8, 128), 0)

    def load(k):
        for copy in loads[k]:
            copy.wait()
        out = []
        for t in range(4):
            parts = [raw[k, v, pl.ds(t, 24, stride=4), :] for v in range(4)]
            out += deal(parts, lane)
        return out

    def pack_cols(planes, source, base, out=None):
        for t, plane in enumerate(planes):
            moved = roll(plane, base + t - source, 1)
            out = moved if out is None else jnp.where(lane == base + t, moved, out)
        return out

    def pack_rows(planes, source, base, out=None):
        for s, plane in enumerate(planes):
            tile = plane[8 * (source // 8):8 * (source // 8) + 8]
            moved = roll(tile, base + s - source % 8, 0)
            out = moved if out is None else jnp.where(sub8 == base + s, moved, out)
        return out

    rw = load(2)
    at_end = jnp.logical_and(lane == 127, col == ncol - 1)
    for t in range(4):
        rw[4 * t + 3] = jnp.where(at_end, 0.0, rw[4 * t + 3])
    dw = load(3)
    at_end = jnp.logical_and(sub == 23, row == nrow - 1)
    for s in range(4):
        dw[12 + s] = jnp.where(at_end, 0.0, dw[12 + s])
    fx = [a * b for a, b in zip(rw, load(0))]
    fy = [a * b for a, b in zip(dw, load(1))]
    s0h[...] = pack_cols(fx[3::4], 127, 124, pack_cols(rw[3::4], 127, 120))
    s0v[...] = pack_rows(fy[12:], 23, 4, pack_rows(dw[12:], 23, 0))
    pl.semaphore_wait(barrier, len(partners))
    phase0 = [
        pltpu.make_async_remote_copy(s0h, g0h, s0_sem.at[0], g0_sem.at[0], device_id=(row, right), device_id_type=MESH),
        pltpu.make_async_remote_copy(s0v, g0v, s0_sem.at[1], g0_sem.at[1], device_id=(down, col), device_id_type=MESH),
    ]
    for copy in phase0:
        copy.start()
    for k in range(16):
        rw_ref[k] = rw[k]
        dw_ref[k] = dw[k]
    anchor = load(4)
    prior = load(5)
    source = [anchor[k] * prior[k] - fx[k] - fy[k] for k in range(16)]
    for copy in phase0:
        copy.wait()

    def shift_left_edge(planes, halo, base):
        return [jnp.where(lane == 0, roll(halo, -(base + t), 1), roll(planes[t], 1, 1)) for t in range(4)]

    def shift_up_edge(planes, halo, base):
        return [
            jnp.where(sub == 0, jnp.broadcast_to(halo[base + s:base + s + 1], shape), roll(planes[s], 1, 0))
            for s in range(4)
        ]

    halo = g0h[...]
    lw0 = shift_left_edge(rw[3::4], halo, 120)
    fl0 = shift_left_edge(fx[3::4], halo, 124)
    halo = g0v[...]
    uw0 = shift_up_edge(dw[12:], halo, 0)
    fu0 = shift_up_edge(fy[12:], halo, 4)
    lw = [lw0[k // 4] if k % 4 == 0 else rw[k - 1] for k in range(16)]
    fl = [fl0[k // 4] if k % 4 == 0 else fx[k - 1] for k in range(16)]
    uw = [uw0[k] if k < 4 else dw[k - 4] for k in range(16)]
    fu = [fu0[k] if k < 4 else fy[k - 4] for k in range(16)]
    diag = [anchor[k] + lw[k] + rw[k] + uw[k] + dw[k] for k in range(16)]
    resid = [source[k] + fl[k] + fu[k] for k in range(16)]
    inv = [1.0 / d for d in diag]
    for k in range(16):
        diag_ref[k] = diag[k]
        inv_ref[k] = inv[k]
        r0_ref[k] = resid[k]
    for k in range(4):
        lw_ref[k] = lw0[k]
        uw_ref[k] = uw0[k]

    def total(planes):
        while len(planes) > 1:
            planes = [a + b for a, b in zip(planes[::2], planes[1::2])]
        return planes[0]

    c_right, c_down = total(rw[3::4]), total(dw[12:])
    c_inv = 1.0 / (total(anchor) + total(lw0) + c_right + total(uw0) + c_down)

    def pack(coarse, planes, h_ref, u_ref, d_ref):
        h, u, d = coarse, coarse[:8], coarse[16:]
        if planes is not None:
            h = pack_cols(planes[3::4], 127, 120, pack_cols(planes[0::4], 0, 4, h))
            u = pack_rows(planes[:4], 0, 4, u)
            d = pack_rows(planes[12:], 23, 0, d)
        h_ref[...] = h
        u_ref[...] = u
        d_ref[...] = d

    def exchange(h, u, d, got_h, got_v, send, recv):
        plan = [(u, got_v.at[0], (up, col)), (u, got_v.at[1], (up, left)), (u, got_v.at[2], (up, right))]
        plan += [(d, got_v.at[3], (down, col)), (d, got_v.at[4], (down, left)), (d, got_v.at[5], (down, right))]
        plan += [(h, got_h.at[0], (row, left)), (h, got_h.at[1], (row, right))]
        plan = [plan[k] for k in (1, 2, 4, 5, 0, 3, 6, 7)]
        out = [
            pltpu.make_async_remote_copy(src, dst, send.at[k], recv.at[k], device_id=who, device_id_type=MESH)
            for k, (src, dst, who) in enumerate(plan)
        ]
        for copy in out:
            copy.start()
        return out

    coarse = total(resid)
    pack(c_right, inv, s1h.at[0], s1u.at[0], s1d.at[0])
    pack(c_down, None, s1h.at[1], s1u.at[1], s1d.at[1])
    pack(c_inv, None, s1h.at[2], s1u.at[2], s1d.at[2])
    pack(coarse, resid, s1h.at[3], s1u.at[3], s1d.at[3])
    copies = exchange(s1h, s1u, s1d, g1h, g1v, sx_sem.at[0], gx_sem.at[0])

    def assemble(own, h, v):
        side = jnp.where(lane < 64, h[0], h[1])
        ring = jnp.where(jnp.logical_or(lane < 4, lane >= 124), side, 0.0)
        below = jnp.where(sub8 < 4, v[0], v[3])
        corner = jnp.where(
            lane8 < 4,
            jnp.where(sub8 < 4, v[1], v[4]),
            jnp.where(lane8 >= 124, jnp.where(sub8 < 4, v[2], v[5]), 0.0),
        )
        ends = jnp.where(sub8 < 4, v[3], v[0])
        ext = jnp.concatenate(
            [jnp.concatenate([own, ring], axis=1), jnp.concatenate([below, corner], axis=1)], axis=0
        )
        return ext, side, ends

    def field(h, v, f=None):
        if f is None:
            return [h[k] for k in range(2)], [v[k] for k in range(6)]
        return [h[k, f] for k in range(2)], [v[k, f] for k in range(6)]

    for copy in copies:
        copy.wait()
    cr, inv_side, inv_ends = assemble(c_right, *field(g1h, g1v, 0))
    cd, _, _ = assemble(c_down, *field(g1h, g1v, 1))
    ci, _, _ = assemble(c_inv, *field(g1h, g1v, 2))
    scale = OMEGA * ci
    a_right, a_left = scale * cr, scale * roll(cr, 1, 1)
    a_down, a_up = scale * cd, scale * roll(cd, 1, 0)

    def smooth(own, h, v):
        ext, side, ends = assemble(own, h, v)
        start = scale * ext
        level = start
        for turn in range(3):
            beside = a_left * roll(level, 1, 1) + a_right * roll(level, -1, 1)
            beside = beside + a_up * roll(level, 1, 0) + a_down * roll(level, -1, 0)
            level = (1.0 - OMEGA) * level + (start + beside)
        e_side, e_ends = level[:24, 128:], level[24:, :128]
        e_side = jnp.where(
            lane < 64, jnp.broadcast_to(e_side[:, 0:1], shape), jnp.broadcast_to(e_side[:, 127:128], shape)
        )
        e_ends = jnp.where(
            sub8 < 4, jnp.broadcast_to(e_ends[7:8], (8, 128)), jnp.broadcast_to(e_ends[0:1], (8, 128))
        )
        return level[:24, :128], inv_side * side + e_side, inv_ends * ends + e_ends

    def operate(v, side, ends, emit):
        west = [jnp.where(lane == 0, roll(side, -(120 + t), 1), roll(v[4 * t + 3], 1, 1)) for t in range(4)]
        east = [jnp.where(lane == 127, roll(side, 127 - (4 + t), 1), roll(v[4 * t], -1, 1)) for t in range(4)]
        north = [
            jnp.where(sub == 0, jnp.broadcast_to(ends[s:s + 1], shape), roll(v[12 + s], 1, 0)) for s in range(4)
        ]
        south = [
            jnp.where(sub == 23, jnp.broadcast_to(ends[4 + s:5 + s], shape), roll(v[s], -1, 0)) for s in range(4)
        ]
        for k in range(16):
            t, s = k // 4, k % 4
            beside = (lw_ref[t] * west[t]) if s == 0 else (rw_ref[k - 1] * v[k - 1])
            beside = beside + rw_ref[k] * (east[t] if s == 3 else v[k + 1])
            beside = beside + ((uw_ref[s] * north[s]) if t == 0 else (dw_ref[k - 4] * v[k - 4]))
            beside = beside + dw_ref[k] * (south[s] if t == 3 else v[k + 4])
            emit(k, diag_ref[k] * v[k] - beside)

    def dot(a, b):
        return total([a[k] * b[k] for k in range(16)])

    sums = {}
    got = field(g1h, g1v, 3)
    source, sides, ends = [resid], None, None
    images, fields = [], []
    for j in range(3):
        if j:
            for copy in copies:
                copy.wait()
            got = field(gh.at[j - 1], gv.at[j - 1])
        level, new_side, new_ends = smooth(coarse, *got)
        if j == 0:
            v = [inv_ref[k] * resid[k] + level for k in range(16)]
            side, ends = new_side, new_ends
        else:
            v = [inv_ref[k] * images[-1][k] + level - fields[-1][k] for k in range(16)]
            side, ends = new_side - side, new_ends - ends
        image = [None] * 16

        def emit(k, value):
            image[k] = value

        operate(v, side, ends, emit)
        for k in range(16):
            u_ref[j, k] = v[k]
            w_ref[j, k] = image[k]
        fields.append(v)
        images.append(image)
        if j < 2:
            coarse = total(image)
            pack(coarse, image, sh.at[j], su.at[j], sd.at[j])
            copies = exchange(sh.at[j], su.at[j], sd.at[j], gh.at[j], gv.at[j], sx_sem.at[j + 1], gx_sem.at[j + 1])
        sums["g", j] = dot(resid, v)
        for i in range(j + 1):
            sums[i, j] = dot(images[i], v)

    order = [("g", 0), ("g", 1), ("g", 2), (0, 0), (0, 1), (0, 2), (1, 1), (1, 2), (2, 2)]
    sums_row = jnp.zeros((1, 128), F)
    lane1 = iota((1, 128), 1)
    for k, name in enumerate(order):
        x8 = sums[name]
        x8 = x8[:8] + x8[8:16] + x8[16:]
        for shift in (64, 32, 16, 8):
            x8 = x8 + roll(x8, shift, 1)
        one = jnp.sum(x8, axis=0, keepdims=True)
        sums_row = jnp.where((lane1 >> 3) == k, one, sums_row)

    base = 0
    for slots, count, me, partner in (
        (slots_a, na, me_a, partner_a), (slots_b, nb, y, partner_b), (slots_c, nc, z, partner_c)
    ):
        part[base] = sums_row
        copies = []
        for k in range(1, count):
            copies.append(pltpu.make_async_remote_copy(
                part.at[base], slots.at[k], sr_sem.at[base, k], gr_sem.at[base, k],
                device_id=partner(k), device_id_type=MESH,
            ))
            copies[-1].start()
        for copy in copies:
            copy.wait()
        sums_row = total_any([sums_row] + [slots[k] for k in range(1, count)])
        base += 1

    for shift in (4, 2, 1):
        sums_row = sums_row + roll(sums_row, -shift, 1)
    value = {
        name: jnp.broadcast_to(sums_row[:, 8 * k:8 * k + 1], (1, 128)) for k, name in enumerate(order)
    }
    g0, g1, g2 = (value["g", j] for j in range(3))
    a00, a01, a02 = value[0, 0], value[0, 1], value[0, 2]
    l10, l20 = a01 / a00, a02 / a00
    d1, t12 = value[1, 1] - l10 * a01, value[1, 2] - l10 * a02
    l21 = t12 / d1
    d2 = value[2, 2] - l20 * a02 - l21 * t12
    y1 = g1 - l10 * g0
    y2 = g2 - l20 * g0 - l21 * y1
    c2 = y2 / d2
    c1 = y1 / d1 - l21 * c2
    c0 = g0 / a00 - l10 * c1 - l20 * c2
    c = [jnp.broadcast_to(v, shape) for v in (c0, c1, c2)]

    stores = []
    for n, out_ref in enumerate((heights_ref, resid_ref)):
        for t in range(4):
            planes = []
            for k in range(4 * t, 4 * t + 4):
                if n == 0:
                    planes.append(c[0] * u_ref[0, k] + c[1] * u_ref[1, k] + c[2] * u_ref[2, k])
                else:
                    planes.append(r0_ref[k] - (c[0] * w_ref[0, k] + c[1] * w_ref[1, k] + c[2] * w_ref[2, k]))
            for v, value in enumerate(undeal(planes, lane)):
                done[n, v, pl.ds(t, 24, stride=4), :] = value
        for v in range(4):
            stores.append(
                pltpu.make_async_copy(done.at[n, v], out_ref.at[:, 128 * v:128 * v + 128], out_sem.at[n, v])
            )
            stores[-1].start()
    for copy in stores:
        copy.wait()


def total_any(values):
    while len(values) > 1:
        rest = values[len(values) // 2 * 2:]
        values = [a + b for a, b in zip(values[::2], values[1::2])] + rest
    return values[0]


def solution(mesh, split=SPLIT):
    na, nb, nc = split["x"] * split["core"], split["y"], split["zh"] * split["zl"]

    def step(*args):
        rows, cols = args[0].shape
        assert (rows, cols) == (96, 512)
        tile, planes = pltpu.VMEM((24, 128), F), pltpu.VMEM((16, 24, 128), F)
        dma = pltpu.SemaphoreType.DMA
        most = max(na, nb, nc)
        out = pl.pallas_call(
            functools.partial(kernel, split),
            out_shape=[jax.ShapeDtypeStruct((rows, cols), F)] * 2,
            in_specs=[pl.BlockSpec(memory_space=pltpu.HBM)] * 6,
            out_specs=[pl.BlockSpec(memory_space=pltpu.HBM)] * 2,
            scratch_shapes=[
                pltpu.VMEM((6, 4, rows, 128), F),
                planes, planes, planes, planes,
                pltpu.VMEM((4, 24, 128), F), pltpu.VMEM((4, 24, 128), F),
                planes,
                pltpu.VMEM((3, 16, 24, 128), F), pltpu.VMEM((3, 16, 24, 128), F),
                tile, pltpu.VMEM((8, 128), F), tile, pltpu.VMEM((8, 128), F),
                pltpu.VMEM((4, 24, 128), F), pltpu.VMEM((4, 8, 128), F), pltpu.VMEM((4, 8, 128), F),
                pltpu.VMEM((2, 4, 24, 128), F), pltpu.VMEM((6, 4, 8, 128), F),
                pltpu.VMEM((2, 24, 128), F), pltpu.VMEM((2, 8, 128), F), pltpu.VMEM((2, 8, 128), F),
                pltpu.VMEM((2, 2, 24, 128), F), pltpu.VMEM((2, 6, 8, 128), F),
                pltpu.VMEM((3, 1, 128), F),
                pltpu.VMEM((na, 1, 128), F), pltpu.VMEM((nb, 1, 128), F), pltpu.VMEM((nc, 1, 128), F),
                pltpu.VMEM((2, 4, rows, 128), F),
                dma((6, 4)), dma((2, 4)), dma((2,)), dma((2,)), dma((3, 8)), dma((3, 8)), dma((3, most)), dma((3, most)),
            ],
            compiler_params=pltpu.CompilerParams(collective_id=0, has_side_effects=True),
        )(*args)
        return tuple(out)

    return jax.shard_map(
        step,
        mesh=mesh,
        in_specs=(P("row", "col"),) * 6,
        out_specs=(P("row", "col"),) * 2,
        check_vma=False,
    )
```

```python
import functools

import jax
import jax.numpy as jnp
from jax import lax
from jax.experimental import pallas as pl
from jax.experimental.pallas import tpu as pltpu
from jax.sharding import PartitionSpec as P

MESH = pl.DeviceIdType.MESH
F = jnp.float32
OMEGA = 2.0 / 3.0

SPLIT = dict(y=8, zh=4, core=2, zl=2, x=4)


def iota(shape, dim):
    return lax.broadcasted_iota(jnp.int32, shape, dim)


def pick(masks, values):
    out = values[-1]
    for mask, value in zip(masks[:-1][::-1], values[:-1][::-1]):
        out = jnp.where(mask, value, out)
    return out


def lane_gather(x, index):
    return jnp.take_along_axis(x, index, axis=1, mode="promise_in_bounds")


def deal(parts, lane):
    low = [(lane & 3) == q for q in range(4)]
    block = [(lane >> 5) == v for v in range(4)]
    moved = []
    for d in range(4):
        merged = pick([low[(v + d) & 3] for v in range(4)], parts)
        moved.append(lane_gather(merged, 4 * (lane & 31) + (((lane >> 5) + d) & 3)))
    return [pick(block, [moved[(s - v) & 3] for v in range(4)]) for s in range(4)]


def undeal(planes, lane):
    low = [(lane & 3) == q for q in range(4)]
    block = [(lane >> 5) == v for v in range(4)]
    moved = []
    for d in range(4):
        merged = pick(block, [planes[(v + d) & 3] for v in range(4)])
        moved.append(lane_gather(merged, 32 * (((lane & 3) - d) & 3) + (lane >> 2)))
    return [pick(low, [moved[(q - v) & 3] for q in range(4)]) for v in range(4)]


def roll(x, shift, axis):
    shift = shift % x.shape[axis]
    return pltpu.roll(x, shift, axis) if shift else x


def kernel(split, *refs):
    ny, nzh, ncore, nzl, nx = (split[k] for k in ("y", "zh", "core", "zl", "x"))
    nrow, ncol = ny * nzh * ncore, nzl * nx
    inputs, refs = refs[:6], refs[6:]
    r0_ref, u_ref, w_ref, c_ref = refs[:4]
    (raw, rw_ref, dw_ref, diag_ref, inv_ref, lw_ref, uw_ref,
     sent0, got0, s1h, s1u, s1d, got1, sh, su, sd, got,
     part, slots_a, slots_b, slots_c,
     in_sem, s0_sem, g0_sem, sx_sem, gx_sem, sr_sem, gr_sem) = refs[4:]

    row, col = lax.axis_index("row"), lax.axis_index("col")
    up, down = lax.rem(row + nrow - 1, nrow), lax.rem(row + 1, nrow)
    left, right = lax.rem(col + ncol - 1, ncol), lax.rem(col + 1, ncol)
    neighbours = [(up, col), (up, left), (up, right), (down, col), (down, left), (down, right), (row, left), (row, right)]

    y, zh, core = row // (nzh * ncore), lax.rem(row // ncore, nzh), lax.rem(row, ncore)
    zl, x = col // nx, lax.rem(col, nx)
    z = zh * nzl + zl

    def device(y, z, core, x):
        return ((y * nzh + z // nzl) * ncore + core, lax.rem(z, nzl) * nx + x)

    na, nb, nc = nx * ncore, ny, nzh * nzl
    me_a = x * ncore + core

    def partner_a(k):
        other = lax.rem(me_a + k, na)
        return device(y, z, lax.rem(other, ncore), other // ncore)

    def partner_b(k):
        return device(lax.rem(y + k, ny), z, core, x)

    def partner_c(k):
        return device(y, lax.rem(z + k, nc), core, x)

    loads = [
        [pltpu.make_async_copy(src.at[:, 128 * v:128 * v + 128], raw.at[k, v], in_sem.at[k]) for v in range(4)]
        for k, src in enumerate(inputs)
    ]
    for k in (2, 3, 0, 1, 4, 5):
        for copy in loads[k]:
            copy.start()

    partners = neighbours + [partner_a(k) for k in range(1, na)]
    partners += [partner_b(k) for k in range(1, nb)] + [partner_c(k) for k in range(1, nc)]
    barrier = pltpu.get_barrier_semaphore()
    for who in partners:
        pl.semaphore_signal(barrier, inc=1, device_id=who, device_id_type=MESH)

    def finish(ref, sem):
        pltpu.make_async_copy(ref, ref, sem).wait()

    shape = (24, 128)
    lane, sub = iota(shape, 1), iota(shape, 0)
    lane8, sub8 = iota((8, 128), 1), iota((8, 128), 0)

    def load(k):
        finish(raw.at[k], in_sem.at[k])
        out = []
        for t in range(4):
            parts = [raw[k, v, pl.ds(t, 24, stride=4), :] for v in range(4)]
            out += deal(parts, lane)
        return out

    def pack_cols(planes, source, base, out=None):
        for t, plane in enumerate(planes):
            moved = roll(plane, base + t - source, 1)
            out = moved if out is None else jnp.where(lane == base + t, moved, out)
        return out

    def pack_rows(planes, source, base, out=None):
        for s, plane in enumerate(planes):
            tile = plane[8 * (source // 8):8 * (source // 8) + 8]
            moved = roll(tile, base + s - source % 8, 0)
            out = moved if out is None else jnp.where(sub8 == base + s, moved, out)
        return out

    rw = load(2)
    at_end = jnp.logical_and(lane == 127, col == ncol - 1)
    for t in range(4):
        rw[4 * t + 3] = jnp.where(at_end, 0.0, rw[4 * t + 3])
    dw = load(3)
    at_end = jnp.logical_and(sub == 23, row == nrow - 1)
    for s in range(4):
        dw[12 + s] = jnp.where(at_end, 0.0, dw[12 + s])
    fx = [a * b for a, b in zip(rw, load(0))]
    fy = [a * b for a, b in zip(dw, load(1))]
    sent0[:3] = pack_cols(fx[3::4], 127, 124, pack_cols(rw[3::4], 127, 120)).reshape(3, 8, 128)
    sent0[3] = pack_rows(fy[12:], 23, 4, pack_rows(dw[12:], 23, 0))
    pl.semaphore_wait(barrier, len(partners))
    for part0, who in ((pl.ds(0, 3), (row, right)), (pl.ds(3, 1), (down, col))):
        pltpu.make_async_remote_copy(
            sent0.at[part0], got0.at[part0], s0_sem, g0_sem, device_id=who, device_id_type=MESH
        ).start()
    for k in range(16):
        rw_ref[k] = rw[k]
        dw_ref[k] = dw[k]
    anchor = load(4)
    prior = load(5)
    source = [anchor[k] * prior[k] - fx[k] - fy[k] for k in range(16)]
    finish(got0, g0_sem)

    def shift_left_edge(planes, halo, base):
        return [jnp.where(lane == 0, roll(halo, -(base + t), 1), roll(planes[t], 1, 1)) for t in range(4)]

    def shift_up_edge(planes, halo, base):
        return [
            jnp.where(sub == 0, jnp.broadcast_to(halo[base + s:base + s + 1], shape), roll(planes[s], 1, 0))
            for s in range(4)
        ]

    halo = got0[:3].reshape(shape)
    lw0 = shift_left_edge(rw[3::4], halo, 120)
    fl0 = shift_left_edge(fx[3::4], halo, 124)
    halo = got0[3]
    uw0 = shift_up_edge(dw[12:], halo, 0)
    fu0 = shift_up_edge(fy[12:], halo, 4)
    lw = [lw0[k // 4] if k % 4 == 0 else rw[k - 1] for k in range(16)]
    fl = [fl0[k // 4] if k % 4 == 0 else fx[k - 1] for k in range(16)]
    uw = [uw0[k] if k < 4 else dw[k - 4] for k in range(16)]
    fu = [fu0[k] if k < 4 else fy[k - 4] for k in range(16)]
    diag = [anchor[k] + lw[k] + rw[k] + uw[k] + dw[k] for k in range(16)]
    resid = [source[k] + fl[k] + fu[k] for k in range(16)]
    inv = [1.0 / d for d in diag]
    for k in range(16):
        diag_ref[k] = diag[k]
        inv_ref[k] = inv[k]
        r0_ref[k] = resid[k]
    for k in range(4):
        lw_ref[k] = lw0[k]
        uw_ref[k] = uw0[k]

    def total(planes):
        while len(planes) > 1:
            planes = [a + b for a, b in zip(planes[::2], planes[1::2])]
        return planes[0]

    c_right, c_down = total(rw[3::4]), total(dw[12:])
    c_inv = 1.0 / (total(anchor) + total(lw0) + c_right + total(uw0) + c_down)

    def pack(coarse, planes, h_ref, u_ref, d_ref):
        h, u, d = coarse, coarse[:8], coarse[16:]
        if planes is not None:
            h = pack_cols(planes[3::4], 127, 120, pack_cols(planes[0::4], 0, 4, h))
            u = pack_rows(planes[:4], 0, 4, u)
            d = pack_rows(planes[12:], 23, 0, d)
        h_ref[...] = h.reshape(3, 8, 128)
        u_ref[0] = u
        d_ref[0] = d

    def exchange(h, u, d, got, n, send, recv):
        plan = [(u, 1, (up, left)), (u, 2, (up, right)), (d, 4, (down, left)), (d, 5, (down, right))]
        plan += [(u, 0, (up, col)), (d, 3, (down, col))]
        plan = [(src, got.at[pl.ds((6 + slot) * n, n)], who) for src, slot, who in plan]
        plan += [(h, got.at[pl.ds(0, 3 * n)], (row, left)), (h, got.at[pl.ds(3 * n, 3 * n)], (row, right))]
        for src, dst, who in plan:
            pltpu.make_async_remote_copy(src, dst, send, recv, device_id=who, device_id_type=MESH).start()

    coarse = total(resid)
    pack(c_right, inv, s1h.at[pl.ds(0, 3)], s1u.at[pl.ds(0, 1)], s1d.at[pl.ds(0, 1)])
    pack(c_down, None, s1h.at[pl.ds(3, 3)], s1u.at[pl.ds(1, 1)], s1d.at[pl.ds(1, 1)])
    pack(c_inv, None, s1h.at[pl.ds(6, 3)], s1u.at[pl.ds(2, 1)], s1d.at[pl.ds(2, 1)])
    pack(coarse, resid, s1h.at[pl.ds(9, 3)], s1u.at[pl.ds(3, 1)], s1d.at[pl.ds(3, 1)])
    exchange(s1h, s1u, s1d, got1, 4, sx_sem.at[0], gx_sem.at[0])

    def assemble(own, h, v):
        side = jnp.where(lane < 64, h[0], h[1])
        ring = jnp.where(jnp.logical_or(lane < 4, lane >= 124), side, 0.0)
        below = jnp.where(sub8 < 4, v[0], v[3])
        corner = jnp.where(
            lane8 < 4,
            jnp.where(sub8 < 4, v[1], v[4]),
            jnp.where(lane8 >= 124, jnp.where(sub8 < 4, v[2], v[5]), 0.0),
        )
        ends = jnp.where(sub8 < 4, v[3], v[0])
        ext = jnp.concatenate(
            [jnp.concatenate([own, ring], axis=1), jnp.concatenate([below, corner], axis=1)], axis=0
        )
        return ext, side, ends

    def field(ref, n, f):
        h = [ref[pl.ds(3 * (n * k + f), 3)].reshape(shape) for k in range(2)]
        return h, [ref[n * (6 + k) + f] for k in range(6)]

    finish(got1, gx_sem.at[0])
    cr, inv_side, inv_ends = assemble(c_right, *field(got1, 4, 0))
    cd, _, _ = assemble(c_down, *field(got1, 4, 1))
    ci, _, _ = assemble(c_inv, *field(got1, 4, 2))
    scale = OMEGA * ci
    a_right, a_left = scale * cr, scale * roll(cr, 1, 1)
    a_down, a_up = scale * cd, scale * roll(cd, 1, 0)

    def smooth(own, h, v):
        ext, side, ends = assemble(own, h, v)
        start = scale * ext
        level = start
        for turn in range(3):
            beside = a_left * roll(level, 1, 1) + a_right * roll(level, -1, 1)
            beside = beside + a_up * roll(level, 1, 0) + a_down * roll(level, -1, 0)
            level = (1.0 - OMEGA) * level + (start + beside)
        e_side, e_ends = level[:24, 128:], level[24:, :128]
        e_side = jnp.where(
            lane < 64, jnp.broadcast_to(e_side[:, 0:1], shape), jnp.broadcast_to(e_side[:, 127:128], shape)
        )
        e_ends = jnp.where(
            sub8 < 4, jnp.broadcast_to(e_ends[7:8], (8, 128)), jnp.broadcast_to(e_ends[0:1], (8, 128))
        )
        return level[:24, :128], inv_side * side + e_side, inv_ends * ends + e_ends

    def operate(v, side, ends, emit):
        west = [jnp.where(lane == 0, roll(side, -(120 + t), 1), roll(v[4 * t + 3], 1, 1)) for t in range(4)]
        east = [jnp.where(lane == 127, roll(side, 127 - (4 + t), 1), roll(v[4 * t], -1, 1)) for t in range(4)]
        north = [
            jnp.where(sub == 0, jnp.broadcast_to(ends[s:s + 1], shape), roll(v[12 + s], 1, 0)) for s in range(4)
        ]
        south = [
            jnp.where(sub == 23, jnp.broadcast_to(ends[4 + s:5 + s], shape), roll(v[s], -1, 0)) for s in range(4)
        ]
        for k in range(16):
            t, s = k // 4, k % 4
            beside = (lw_ref[t] * west[t]) if s == 0 else (rw_ref[k - 1] * v[k - 1])
            beside = beside + rw_ref[k] * (east[t] if s == 3 else v[k + 1])
            beside = beside + ((uw_ref[s] * north[s]) if t == 0 else (dw_ref[k - 4] * v[k - 4]))
            beside = beside + dw_ref[k] * (south[s] if t == 3 else v[k + 4])
            emit(k, diag_ref[k] * v[k] - beside)

    def dot(a, b):
        return total([a[k] * b[k] for k in range(16)])

    sums = {}
    news = field(got1, 4, 3)
    images, fields = [], []
    for j in range(3):
        if j:
            finish(got.at[j - 1], gx_sem.at[j])
            news = field(got.at[j - 1], 1, 0)
        level, new_side, new_ends = smooth(coarse, *news)
        if j == 0:
            v = [inv_ref[k] * resid[k] + level for k in range(16)]
            side, ends = new_side, new_ends
        else:
            v = [inv_ref[k] * images[-1][k] + level - fields[-1][k] for k in range(16)]
            side, ends = new_side - side, new_ends - ends
        image = [None] * 16

        def emit(k, value):
            image[k] = value

        operate(v, side, ends, emit)
        for k in range(16):
            u_ref[j, k] = v[k]
            w_ref[j, k] = image[k]
        fields.append(v)
        images.append(image)
        if j < 2:
            coarse = total(image)
            pack(coarse, image, sh.at[j], su.at[j], sd.at[j])
            exchange(sh.at[j], su.at[j], sd.at[j], got.at[j], 1, sx_sem.at[j + 1], gx_sem.at[j + 1])
        sums["g", j] = dot(resid, v)
        for i in range(j + 1):
            sums[i, j] = dot(images[i], v)

    order = [("g", 0), ("g", 1), ("g", 2), (0, 0), (0, 1), (0, 2), (1, 1), (1, 2), (2, 2)]
    sums_row = jnp.zeros((1, 128), F)
    lane1 = iota((1, 128), 1)
    for k, name in enumerate(order):
        x8 = sums[name]
        x8 = x8[:8] + x8[8:16] + x8[16:]
        for shift in (64, 32, 16, 8):
            x8 = x8 + roll(x8, shift, 1)
        one = jnp.sum(x8, axis=0, keepdims=True)
        sums_row = jnp.where((lane1 >> 3) == k, one, sums_row)

    base = 0
    for slots, count, me, partner in (
        (slots_a, na, me_a, partner_a), (slots_b, nb, y, partner_b), (slots_c, nc, z, partner_c)
    ):
        part[base] = sums_row
        for k in range(1, count):
            pltpu.make_async_remote_copy(
                part.at[base], slots.at[k], sr_sem.at[base], gr_sem.at[base], device_id=partner(k), device_id_type=MESH
            ).start()
        if count > 1:
            finish(slots.at[pl.ds(1, count - 1)], gr_sem.at[base])
        sums_row = total_any([sums_row] + [slots[k] for k in range(1, count)])
        base += 1

    for shift in (4, 2, 1):
        sums_row = sums_row + roll(sums_row, -shift, 1)
    value = {
        name: jnp.broadcast_to(sums_row[:, 8 * k:8 * k + 1], (1, 128)) for k, name in enumerate(order)
    }
    g0, g1, g2 = (value["g", j] for j in range(3))
    a00, a01, a02 = value[0, 0], value[0, 1], value[0, 2]
    l10, l20 = a01 / a00, a02 / a00
    d1, t12 = value[1, 1] - l10 * a01, value[1, 2] - l10 * a02
    l21 = t12 / d1
    d2 = value[2, 2] - l20 * a02 - l21 * t12
    y1 = g1 - l10 * g0
    y2 = g2 - l20 * g0 - l21 * y1
    c2 = y2 / d2
    c1 = y1 / d1 - l21 * c2
    c0 = g0 / a00 - l10 * c1 - l20 * c2
    for k, value in enumerate((c0, c1, c2)):
        c_ref[k] = jnp.broadcast_to(value, (8, 128))

    finish(sent0, s0_sem)
    finish(got1, sx_sem.at[0])
    for j in range(2):
        finish(got.at[j], sx_sem.at[j + 1])
    for k, slots in enumerate((slots_a, slots_b, slots_c)):
        if slots.shape[0] > 1:
            finish(slots.at[pl.ds(1, slots.shape[0] - 1)], sr_sem.at[k])


def combine(r0_ref, u_ref, w_ref, c_ref, heights_ref, resid_ref, done, sem):
    lane = iota((24, 128), 1)
    c = [jnp.concatenate([c_ref[k]] * 3, axis=0) for k in range(3)]
    for n, out_ref in enumerate((heights_ref, resid_ref)):
        for t in range(4):
            planes = []
            for k in range(4 * t, 4 * t + 4):
                if n == 0:
                    planes.append(c[0] * u_ref[0, k] + c[1] * u_ref[1, k] + c[2] * u_ref[2, k])
                else:
                    planes.append(r0_ref[k] - (c[0] * w_ref[0, k] + c[1] * w_ref[1, k] + c[2] * w_ref[2, k]))
            for v, value in enumerate(undeal(planes, lane)):
                done[n, v, pl.ds(t, 24, stride=4), :] = value
        for v in range(4):
            pltpu.make_async_copy(done.at[n, v], out_ref.at[:, 128 * v:128 * v + 128], sem.at[n]).start()
    for n in range(2):
        pltpu.make_async_copy(done.at[n], done.at[n], sem.at[n]).wait()


def total_any(values):
    while len(values) > 1:
        rest = values[len(values) // 2 * 2:]
        values = [a + b for a, b in zip(values[::2], values[1::2])] + rest
    return values[0]


def solution(mesh, split=SPLIT):
    na, nb, nc = split["x"] * split["core"], split["y"], split["zh"] * split["zl"]

    def step(*args):
        rows, cols = args[0].shape
        assert (rows, cols) == (96, 512)
        shapes = [(16, 24, 128), (3, 16, 24, 128), (3, 16, 24, 128), (3, 8, 128)]
        dma = pltpu.SemaphoreType.DMA

        def vmem(*shape):
            return pltpu.VMEM(shape, F)

        args = [pltpu.with_memory_space_constraint(x, pltpu.HBM) for x in args]
        parts = pl.pallas_call(
            functools.partial(kernel, split),
            out_shape=[jax.ShapeDtypeStruct(shape, F) for shape in shapes],
            in_specs=[pl.BlockSpec(memory_space=pltpu.HBM)] * 6,
            out_specs=[pl.BlockSpec(memory_space=pltpu.VMEM)] * 4,
            scratch_shapes=[
                vmem(6, 4, rows, 128),
                vmem(16, 24, 128), vmem(16, 24, 128), vmem(16, 24, 128), vmem(16, 24, 128),
                vmem(4, 24, 128), vmem(4, 24, 128),
                vmem(4, 8, 128), vmem(4, 8, 128),
                vmem(12, 8, 128), vmem(4, 8, 128), vmem(4, 8, 128), vmem(48, 8, 128),
                vmem(2, 3, 8, 128), vmem(2, 1, 8, 128), vmem(2, 1, 8, 128), vmem(2, 12, 8, 128),
                vmem(3, 1, 128), vmem(na, 1, 128), vmem(nb, 1, 128), vmem(nc, 1, 128),
                dma((6,)), dma(()), dma(()), dma((3,)), dma((3,)), dma((3,)), dma((3,)),
            ],
            compiler_params=pltpu.CompilerParams(
                collective_id=0, has_side_effects=True, vmem_limit_bytes=12 * 2**20
            ),
        )(*args)
        return tuple(pl.pallas_call(
            combine,
            out_shape=[jax.ShapeDtypeStruct((rows, cols), F)] * 2,
            in_specs=[pl.BlockSpec(memory_space=pltpu.VMEM)] * 4,
            out_specs=[pl.BlockSpec(memory_space=pltpu.HBM)] * 2,
            scratch_shapes=[vmem(2, 4, rows, 128), dma((2,))],
            compiler_params=pltpu.CompilerParams(vmem_limit_bytes=12 * 2**20),
        )(*parts))

    return jax.shard_map(
        step,
        mesh=mesh,
        in_specs=(P("row", "col"),) * 6,
        out_specs=(P("row", "col"),) * 2,
        check_vma=False,
    )
```

```python
import functools

import jax
import jax.numpy as jnp
from jax import lax
from jax.experimental import pallas as pl
from jax.experimental.pallas import tpu as pltpu
from jax.sharding import PartitionSpec as P

MESH = pl.DeviceIdType.MESH
F = jnp.float32
OMEGA = 2.0 / 3.0

SPLIT = dict(y=8, zh=4, core=2, zl=2, x=4)


def iota(shape, dim):
    return lax.broadcasted_iota(jnp.int32, shape, dim)


def pick(masks, values):
    out = values[-1]
    for mask, value in zip(masks[:-1][::-1], values[:-1][::-1]):
        out = jnp.where(mask, value, out)
    return out


def lane_gather(x, index):
    return jnp.take_along_axis(x, index, axis=1, mode="promise_in_bounds")


def deal(parts, lane):
    low = [(lane & 3) == q for q in range(4)]
    block = [(lane >> 5) == v for v in range(4)]
    moved = []
    for d in range(4):
        merged = pick([low[(v + d) & 3] for v in range(4)], parts)
        moved.append(lane_gather(merged, 4 * (lane & 31) + (((lane >> 5) + d) & 3)))
    return [pick(block, [moved[(s - v) & 3] for v in range(4)]) for s in range(4)]


def undeal(planes, lane):
    low = [(lane & 3) == q for q in range(4)]
    block = [(lane >> 5) == v for v in range(4)]
    moved = []
    for d in range(4):
        merged = pick(block, [planes[(v + d) & 3] for v in range(4)])
        moved.append(lane_gather(merged, 32 * (((lane & 3) - d) & 3) + (lane >> 2)))
    return [pick(low, [moved[(q - v) & 3] for q in range(4)]) for v in range(4)]


def roll(x, shift, axis):
    shift = shift % x.shape[axis]
    return pltpu.roll(x, shift, axis) if shift else x


def kernel(split, *refs):
    ny, nzh, ncore, nzl, nx = (split[k] for k in ("y", "zh", "core", "zl", "x"))
    nrow, ncol = ny * nzh * ncore, nzl * nx
    inputs, refs = refs[:6], refs[6:]
    r0_ref, u_ref, w_ref, c_ref = refs[:4]
    (raw, rw_ref, dw_ref, diag_ref, inv_ref, lw_ref, uw_ref,
     s1h, s1u, s1d, got1, sh, su, sd, got,
     part, slots_a, slots_b, slots_c,
     in_sem, sx_sem, gx_sem, sr_sem, gr_sem) = refs[4:]

    row, col = lax.axis_index("row"), lax.axis_index("col")
    up, down = lax.rem(row + nrow - 1, nrow), lax.rem(row + 1, nrow)
    left, right = lax.rem(col + ncol - 1, ncol), lax.rem(col + 1, ncol)
    neighbours = [(up, col), (up, left), (up, right), (down, col), (down, left), (down, right), (row, left), (row, right)]

    y, zh, core = row // (nzh * ncore), lax.rem(row // ncore, nzh), lax.rem(row, ncore)
    zl, x = col // nx, lax.rem(col, nx)
    z = zh * nzl + zl

    def device(y, z, core, x):
        return ((y * nzh + z // nzl) * ncore + core, lax.rem(z, nzl) * nx + x)

    na, nb, nc = nx * ncore, ny, nzh * nzl
    me_a = x * ncore + core

    def partner_a(k):
        other = lax.rem(me_a + k, na)
        return device(y, z, lax.rem(other, ncore), other // ncore)

    def partner_b(k):
        return device(lax.rem(y + k, ny), z, core, x)

    def partner_c(k):
        return device(y, lax.rem(z + k, nc), core, x)

    loads = [
        [pltpu.make_async_copy(src.at[:, 128 * v:128 * v + 128], raw.at[k, v], in_sem.at[k]) for v in range(4)]
        for k, src in enumerate(inputs)
    ]
    for k in (2, 3, 0, 1, 4, 5):
        for copy in loads[k]:
            copy.start()

    partners = neighbours + [partner_a(k) for k in range(1, na)]
    partners += [partner_b(k) for k in range(1, nb)] + [partner_c(k) for k in range(1, nc)]
    barrier = pltpu.get_barrier_semaphore()
    for who in partners:
        pl.semaphore_signal(barrier, inc=1, device_id=who, device_id_type=MESH)

    def finish(ref, sem):
        pltpu.make_async_copy(ref, ref, sem).wait()

    shape = (24, 128)
    lane, sub = iota(shape, 1), iota(shape, 0)
    lane8, sub8 = iota((8, 128), 1), iota((8, 128), 0)

    def load(k):
        finish(raw.at[k], in_sem.at[k])
        out = []
        for t in range(4):
            parts = [raw[k, v, pl.ds(t, 24, stride=4), :] for v in range(4)]
            out += deal(parts, lane)
        return out

    def pack_cols(planes, source, base, out=None):
        for t, plane in enumerate(planes):
            moved = roll(plane, base + t - source, 1)
            out = moved if out is None else jnp.where(lane == base + t, moved, out)
        return out

    def pack_rows(planes, source, base, out=None):
        for s, plane in enumerate(planes):
            tile = plane[8 * (source // 8):8 * (source // 8) + 8]
            moved = roll(tile, base + s - source % 8, 0)
            out = moved if out is None else jnp.where(sub8 == base + s, moved, out)
        return out

    rw = load(2)
    at_end = jnp.logical_and(lane == 127, col == ncol - 1)
    for t in range(4):
        rw[4 * t + 3] = jnp.where(at_end, 0.0, rw[4 * t + 3])
    dw = load(3)
    at_end = jnp.logical_and(sub == 23, row == nrow - 1)
    for s in range(4):
        dw[12 + s] = jnp.where(at_end, 0.0, dw[12 + s])
    fx = [a * b for a, b in zip(rw, load(0))]
    fy = [a * b for a, b in zip(dw, load(1))]
    anchor = load(4)
    prior = load(5)

    def behind(planes):
        return [jnp.where(lane == 0, 0.0, roll(planes[4 * t + 3], 1, 1)) for t in range(4)]

    def above(planes):
        return [jnp.where(sub == 0, 0.0, roll(planes[12 + s], 1, 0)) for s in range(4)]

    def spread(first, planes, step):
        if step == 1:
            return [first[k // 4] if k % 4 == 0 else planes[k - 1] for k in range(16)]
        return [first[k] if k < 4 else planes[k - 4] for k in range(16)]

    lw0, fl0, uw0, fu0 = behind(rw), behind(fx), above(dw), above(fy)
    lw, fl, uw, fu = spread(lw0, rw, 1), spread(fl0, fx, 1), spread(uw0, dw, 4), spread(fu0, fy, 4)
    diag = [anchor[k] + lw[k] + rw[k] + uw[k] + dw[k] for k in range(16)]
    resid = [anchor[k] * prior[k] - fx[k] - fy[k] + fl[k] + fu[k] for k in range(16)]

    def total(planes):
        while len(planes) > 1:
            planes = [a + b for a, b in zip(planes[::2], planes[1::2])]
        return planes[0]

    c_right, c_down = total(rw[3::4]), total(dw[12:])
    c_diag = total(anchor) + total(lw0) + c_right + total(uw0) + c_down
    c_resid, c_fx, c_fy = total(resid), total(fx[3::4]), total(fy[12:])

    def side_tile(coarse, planes=None, edge=None):
        h = coarse
        if planes is not None:
            h = pack_cols(planes[3::4], 127, 120, pack_cols(planes[0::4], 0, 4, h))
        if edge is not None:
            h = pack_cols(edge[3::4], 127, 116, h)
        return h

    h0, h1 = side_tile(c_right, diag, rw), side_tile(c_down, resid, fx)
    h2 = jnp.where(lane == 119, roll(c_fx, -8, 1), c_diag)
    h3 = jnp.where(
        jnp.logical_and(lane >= 4, lane < 8), roll(c_fy, 4, 1),
        jnp.where(jnp.logical_and(lane >= 120, lane < 124), roll(c_fy, -4, 1), c_resid),
    )
    for k, h in enumerate((h0, h1, h2, h3)):
        s1h[3 * k:3 * k + 3] = h.reshape(3, 8, 128)
    s1u[0] = pack_rows(diag[:4], 0, 4, c_right[:8])
    s1u[1] = pack_rows(resid[:4], 0, 4, c_down[:8])
    s1u[2] = jnp.where(sub8 < 4, c_diag[:8], roll(c_fx[:8], 4, 0))
    s1u[3] = pack_rows([rw[3], fx[3]], 0, 4, c_resid[:8])
    s1d[0] = pack_rows(diag[12:], 23, 0, c_right[16:])
    s1d[1] = pack_rows(resid[12:], 23, 0, c_down[16:])
    s1d[2] = jnp.where(sub8 >= 4, c_diag[16:], roll(c_fx[16:], 4, 0))
    s1d[3] = pack_rows([c_fy, rw[15], fx[15]], 23, 0, c_resid[16:])
    d4 = pack_rows(fy[12:], 23, 4, pack_rows(dw[12:], 23, 0))
    s1d[4] = d4

    def pack(coarse, planes, h_ref, u_ref, d_ref):
        h_ref[...] = side_tile(coarse, planes).reshape(3, 8, 128)
        u_ref[0] = pack_rows(planes[:4], 0, 4, coarse[:8])
        d_ref[0] = pack_rows(planes[12:], 23, 0, coarse[16:])

    def exchange(h, u, d, got, nu, nd, send, recv):
        nh = h.shape[0]
        plan = [(u, 1, (up, left)), (u, 2, (up, right)), (d, 4, (down, left)), (d, 5, (down, right))]
        plan += [(u, 0, (up, col)), (d, 3, (down, col))]
        plan = [
            (src, got.at[pl.ds(2 * nh + (nu * k if k < 3 else 3 * nu + nd * (k - 3)), nu if k < 3 else nd)], who)
            for src, k, who in plan
        ]
        plan += [(h, got.at[pl.ds(0, nh)], (row, left)), (h, got.at[pl.ds(nh, nh)], (row, right))]
        for src, dst, who in plan:
            pltpu.make_async_remote_copy(src, dst, send, recv, device_id=who, device_id_type=MESH).start()

    pl.semaphore_wait(barrier, len(partners))
    exchange(s1h, s1u, s1d, got1, 4, 5, sx_sem.at[0], gx_sem.at[0])
    for k in range(16):
        rw_ref[k] = rw[k]
        dw_ref[k] = dw[k]

    def assemble(own, h, v, fill=0.0):
        side = jnp.where(lane < 64, h[0], h[1])
        ring = jnp.where(jnp.logical_or(lane < 4, lane >= 124), side, fill)
        below = jnp.where(sub8 < 4, v[0], v[3])
        corner = jnp.where(
            lane8 < 4,
            jnp.where(sub8 < 4, v[1], v[4]),
            jnp.where(lane8 >= 124, jnp.where(sub8 < 4, v[2], v[5]), fill),
        )
        ends = jnp.where(sub8 < 4, v[3], v[0])
        return quad(own, ring, below, corner), side, ends

    def quad(own, ring, below, corner):
        return jnp.concatenate(
            [jnp.concatenate([own, ring], axis=1), jnp.concatenate([below, corner], axis=1)], axis=0
        )

    finish(got1, gx_sem.at[0])
    hs = [[got1[pl.ds(12 * k + 3 * f, 3)].reshape(shape) for k in range(2)] for f in range(4)]
    vs = [[got1[24 + 4 * k + f] for k in range(3)] + [got1[36 + 5 * k + f] for k in range(3)] for f in range(4)]
    from_up, from_up_right, from_up_left = (got1[36 + 5 * k + 4] for k in range(3))

    cr, diag_side, diag_ends = assemble(c_right, hs[0], vs[0])
    cd, side, ends = assemble(c_down, hs[1], vs[1])
    cdiag, _, _ = assemble(c_diag, hs[2], vs[2], 1.0)
    ext, _, _ = assemble(c_resid, hs[3], vs[3])

    lane_x, sub_x = iota((32, 256), 1), iota((32, 256), 0)
    first_col = (lane_x & 127) == 0
    first_row = jnp.logical_or(sub_x == 0, sub_x == 24)
    cdiag = cdiag + jnp.where(first_col, roll(cr, 1, 1), 0.0) + jnp.where(first_row, roll(cd, 1, 0), 0.0)
    across = quad(
        roll(hs[2][1], 9, 1),
        roll(c_fx, 1, 1),
        roll(roll(jnp.where(sub8 < 4, vs[2][5], vs[2][2]), 4, 0), 1, 1),
        roll(roll(jnp.where(sub8 < 4, vs[2][3], vs[2][0]), 4, 0), 1, 1),
    )
    ext = ext + jnp.where(first_col, across, 0.0)
    beyond = jnp.where(lane8 < 64, vs[3][4], vs[3][5])
    near = jnp.where(lane < 64, roll(hs[3][0], -4, 1), roll(hs[3][1], 4, 1))
    across = quad(
        jnp.broadcast_to(vs[3][3][0:1], shape),
        jnp.broadcast_to(beyond[0:1], shape),
        roll(c_fy[16:], 1, 0),
        roll(near[16:], 1, 0),
    )
    in_ring = jnp.logical_or(lane_x < 132, lane_x >= 252)
    ext = ext + jnp.where(jnp.logical_and(first_row, in_ring), across, 0.0)

    to_right = jnp.logical_and(lane >= 4, lane < 8)
    to_left = jnp.logical_and(lane >= 120, lane < 124)
    top_right = jnp.logical_and(sub == 0, lane == 4)
    top_left = jnp.logical_and(sub == 0, lane == 120)
    far_right, far_left = roll(from_up_right, 4, 1), roll(from_up_left, -7, 1)
    col_up, col_down = roll(vs[3][5], 1, 1), roll(vs[3][2], 1, 1)
    up_corner = jnp.logical_and(lane8 == 0, sub8 == 0)
    down_corner = jnp.logical_and(lane8 == 0, sub8 == 4)

    def complete(at_side, at_ends, edge, row_edge, n):
        at_side = at_side + jnp.where(to_right, roll(edge, 16, 1), 0.0)
        at_side = at_side + jnp.where(top_right, jnp.broadcast_to(far_right[4 * n:4 * n + 1], shape), 0.0)
        at_side = at_side + jnp.where(top_left, jnp.broadcast_to(far_left[4 * n + 3:4 * n + 4], shape), 0.0)
        at_ends = at_ends + jnp.where(sub8 >= 4, row_edge, 0.0)
        at_ends = at_ends + jnp.where(up_corner, jnp.broadcast_to(col_up[1 + n:2 + n], (8, 128)), 0.0)
        at_ends = at_ends + jnp.where(down_corner, jnp.broadcast_to(col_down[4 + n:5 + n], (8, 128)), 0.0)
        return at_side, at_ends

    diag_side, diag_ends = complete(diag_side, diag_ends, h0, roll(d4, 4, 0), 0)
    side, ends = complete(side, ends, h1, d4, 1)
    inv_side = 1.0 / jnp.where(jnp.logical_or(to_right, to_left), diag_side, 1.0)
    inv_ends = 1.0 / diag_ends

    for t in range(4):
        more = jnp.where(lane == 0, roll(hs[0][1], -(116 + t), 1), 0.0)
        lw0[t] = lw0[t] + more
        diag[4 * t] = diag[4 * t] + more
        resid[4 * t] = resid[4 * t] + jnp.where(lane == 0, roll(hs[1][1], -(116 + t), 1), 0.0)
    for s in range(4):
        more = jnp.where(sub == 0, jnp.broadcast_to(from_up[s:s + 1], shape), 0.0)
        uw0[s] = uw0[s] + more
        diag[s] = diag[s] + more
        resid[s] = resid[s] + jnp.where(sub == 0, jnp.broadcast_to(from_up[4 + s:5 + s], shape), 0.0)
    inv = [1.0 / d for d in diag]
    for k in range(16):
        diag_ref[k] = diag[k]
        inv_ref[k] = inv[k]
        r0_ref[k] = resid[k]
    for k in range(4):
        lw_ref[k] = lw0[k]
        uw_ref[k] = uw0[k]

    scale = OMEGA / cdiag
    a_right, a_left = scale * cr, scale * roll(cr, 1, 1)
    a_down, a_up = scale * cd, scale * roll(cd, 1, 0)

    def smooth(ext, side, ends):
        start = scale * ext
        level = start
        for turn in range(3):
            beside = a_left * roll(level, 1, 1) + a_right * roll(level, -1, 1)
            beside = beside + a_up * roll(level, 1, 0) + a_down * roll(level, -1, 0)
            level = (1.0 - OMEGA) * level + (start + beside)
        e_side, e_ends = level[:24, 128:], level[24:, :128]
        e_side = jnp.where(
            lane < 64, jnp.broadcast_to(e_side[:, 0:1], shape), jnp.broadcast_to(e_side[:, 127:128], shape)
        )
        e_ends = jnp.where(
            sub8 < 4, jnp.broadcast_to(e_ends[7:8], (8, 128)), jnp.broadcast_to(e_ends[0:1], (8, 128))
        )
        return level[:24, :128], inv_side * side + e_side, inv_ends * ends + e_ends

    def operate(v, side, ends, emit):
        west = [jnp.where(lane == 0, roll(side, -(120 + t), 1), roll(v[4 * t + 3], 1, 1)) for t in range(4)]
        east = [jnp.where(lane == 127, roll(side, 127 - (4 + t), 1), roll(v[4 * t], -1, 1)) for t in range(4)]
        north = [
            jnp.where(sub == 0, jnp.broadcast_to(ends[s:s + 1], shape), roll(v[12 + s], 1, 0)) for s in range(4)
        ]
        south = [
            jnp.where(sub == 23, jnp.broadcast_to(ends[4 + s:5 + s], shape), roll(v[s], -1, 0)) for s in range(4)
        ]
        for k in range(16):
            t, s = k // 4, k % 4
            beside = (lw_ref[t] * west[t]) if s == 0 else (rw_ref[k - 1] * v[k - 1])
            beside = beside + rw_ref[k] * (east[t] if s == 3 else v[k + 1])
            beside = beside + ((uw_ref[s] * north[s]) if t == 0 else (dw_ref[k - 4] * v[k - 4]))
            beside = beside + dw_ref[k] * (south[s] if t == 3 else v[k + 4])
            emit(k, diag_ref[k] * v[k] - beside)

    def dot(a, b):
        return total([a[k] * b[k] for k in range(16)])

    sums = {}
    news = ext, side, ends
    images, fields = [], []
    for j in range(3):
        if j:
            finish(got.at[j - 1], gx_sem.at[j])
            news = assemble(
                coarse, [got[j - 1, 3 * k:3 * k + 3].reshape(shape) for k in range(2)], [got[j - 1, 6 + k] for k in range(6)]
            )
        level, new_side, new_ends = smooth(*news)
        if j == 0:
            v = [inv_ref[k] * resid[k] + level for k in range(16)]
            side, ends = new_side, new_ends
        else:
            v = [inv_ref[k] * images[-1][k] + level - fields[-1][k] for k in range(16)]
            side, ends = new_side - side, new_ends - ends
        image = [None] * 16

        def emit(k, value):
            image[k] = value

        operate(v, side, ends, emit)
        for k in range(16):
            u_ref[j, k] = v[k]
            w_ref[j, k] = image[k]
        fields.append(v)
        images.append(image)
        if j < 2:
            coarse = total(image)
            pack(coarse, image, sh.at[j], su.at[j], sd.at[j])
            exchange(sh.at[j], su.at[j], sd.at[j], got.at[j], 1, 1, sx_sem.at[j + 1], gx_sem.at[j + 1])
        sums["g", j] = dot(resid, v)
        for i in range(j + 1):
            sums[i, j] = dot(images[i], v)

    order = [("g", 0), ("g", 1), ("g", 2), (0, 0), (0, 1), (0, 2), (1, 1), (1, 2), (2, 2)]
    sums_row = jnp.zeros((1, 128), F)
    lane1 = iota((1, 128), 1)
    for k, name in enumerate(order):
        x8 = sums[name]
        x8 = x8[:8] + x8[8:16] + x8[16:]
        for shift in (64, 32, 16, 8):
            x8 = x8 + roll(x8, shift, 1)
        one = jnp.sum(x8, axis=0, keepdims=True)
        sums_row = jnp.where((lane1 >> 3) == k, one, sums_row)

    base = 0
    for slots, count, me, partner in (
        (slots_a, na, me_a, partner_a), (slots_b, nb, y, partner_b), (slots_c, nc, z, partner_c)
    ):
        part[base] = sums_row
        for k in range(1, count):
            pltpu.make_async_remote_copy(
                part.at[base], slots.at[k], sr_sem.at[base], gr_sem.at[base], device_id=partner(k), device_id_type=MESH
            ).start()
        if count > 1:
            finish(slots.at[pl.ds(1, count - 1)], gr_sem.at[base])
        sums_row = total_any([sums_row] + [slots[k] for k in range(1, count)])
        base += 1

    for shift in (4, 2, 1):
        sums_row = sums_row + roll(sums_row, -shift, 1)
    value = {
        name: jnp.broadcast_to(sums_row[:, 8 * k:8 * k + 1], (1, 128)) for k, name in enumerate(order)
    }
    g0, g1, g2 = (value["g", j] for j in range(3))
    a00, a01, a02 = value[0, 0], value[0, 1], value[0, 2]
    l10, l20 = a01 / a00, a02 / a00
    d1, t12 = value[1, 1] - l10 * a01, value[1, 2] - l10 * a02
    l21 = t12 / d1
    d2 = value[2, 2] - l20 * a02 - l21 * t12
    y1 = g1 - l10 * g0
    y2 = g2 - l20 * g0 - l21 * y1
    c2 = y2 / d2
    c1 = y1 / d1 - l21 * c2
    c0 = g0 / a00 - l10 * c1 - l20 * c2
    for k, value in enumerate((c0, c1, c2)):
        c_ref[k] = jnp.broadcast_to(value, (8, 128))

    finish(got1, sx_sem.at[0])
    for j in range(2):
        finish(got.at[j], sx_sem.at[j + 1])
    for k, slots in enumerate((slots_a, slots_b, slots_c)):
        if slots.shape[0] > 1:
            finish(slots.at[pl.ds(1, slots.shape[0] - 1)], sr_sem.at[k])


def combine(r0_ref, u_ref, w_ref, c_ref, heights_ref, resid_ref, done, sem):
    lane = iota((24, 128), 1)
    c = [jnp.concatenate([c_ref[k]] * 3, axis=0) for k in range(3)]
    for n, out_ref in enumerate((heights_ref, resid_ref)):
        for t in range(4):
            planes = []
            for k in range(4 * t, 4 * t + 4):
                if n == 0:
                    planes.append(c[0] * u_ref[0, k] + c[1] * u_ref[1, k] + c[2] * u_ref[2, k])
                else:
                    planes.append(r0_ref[k] - (c[0] * w_ref[0, k] + c[1] * w_ref[1, k] + c[2] * w_ref[2, k]))
            for v, value in enumerate(undeal(planes, lane)):
                done[n, v, pl.ds(t, 24, stride=4), :] = value
        for v in range(4):
            pltpu.make_async_copy(done.at[n, v], out_ref.at[:, 128 * v:128 * v + 128], sem.at[n]).start()
    for n in range(2):
        pltpu.make_async_copy(done.at[n], done.at[n], sem.at[n]).wait()


def total_any(values):
    while len(values) > 1:
        rest = values[len(values) // 2 * 2:]
        values = [a + b for a, b in zip(values[::2], values[1::2])] + rest
    return values[0]


def solution(mesh, split=SPLIT):
    na, nb, nc = split["x"] * split["core"], split["y"], split["zh"] * split["zl"]

    def step(*args):
        rows, cols = args[0].shape
        assert (rows, cols) == (96, 512)
        shapes = [(16, 24, 128), (3, 16, 24, 128), (3, 16, 24, 128), (3, 8, 128)]
        dma = pltpu.SemaphoreType.DMA

        def vmem(*shape):
            return pltpu.VMEM(shape, F)

        args = [pltpu.with_memory_space_constraint(x, pltpu.HBM) for x in args]
        parts = pl.pallas_call(
            functools.partial(kernel, split),
            out_shape=[jax.ShapeDtypeStruct(shape, F) for shape in shapes],
            in_specs=[pl.BlockSpec(memory_space=pltpu.HBM)] * 6,
            out_specs=[pl.BlockSpec(memory_space=pltpu.VMEM)] * 4,
            scratch_shapes=[
                vmem(6, 4, rows, 128),
                vmem(16, 24, 128), vmem(16, 24, 128), vmem(16, 24, 128), vmem(16, 24, 128),
                vmem(4, 24, 128), vmem(4, 24, 128),
                vmem(12, 8, 128), vmem(4, 8, 128), vmem(5, 8, 128), vmem(51, 8, 128),
                vmem(2, 3, 8, 128), vmem(2, 1, 8, 128), vmem(2, 1, 8, 128), vmem(2, 12, 8, 128),
                vmem(3, 1, 128), vmem(na, 1, 128), vmem(nb, 1, 128), vmem(nc, 1, 128),
                dma((6,)), dma((3,)), dma((3,)), dma((3,)), dma((3,)),
            ],
            compiler_params=pltpu.CompilerParams(
                collective_id=0, has_side_effects=True, vmem_limit_bytes=12 * 2**20
            ),
        )(*args)
        return tuple(pl.pallas_call(
            combine,
            out_shape=[jax.ShapeDtypeStruct((rows, cols), F)] * 2,
            in_specs=[pl.BlockSpec(memory_space=pltpu.VMEM)] * 4,
            out_specs=[pl.BlockSpec(memory_space=pltpu.HBM)] * 2,
            scratch_shapes=[vmem(2, 4, rows, 128), dma((2,))],
            compiler_params=pltpu.CompilerParams(vmem_limit_bytes=12 * 2**20),
        )(*parts))

    return jax.shard_map(
        step,
        mesh=mesh,
        in_specs=(P("row", "col"),) * 6,
        out_specs=(P("row", "col"),) * 2,
        check_vma=False,
    )
```

```python
import functools

import jax
import jax.numpy as jnp
from jax import lax
from jax.experimental import pallas as pl
from jax.experimental.pallas import tpu as pltpu
from jax.sharding import PartitionSpec as P

MESH = pl.DeviceIdType.MESH
F = jnp.float32
OMEGA = 2.0 / 3.0

SPLIT = dict(y=8, zh=4, core=2, zl=2, x=4)


def iota(shape, dim):
    return lax.broadcasted_iota(jnp.int32, shape, dim)


def pick(masks, values):
    out = values[-1]
    for mask, value in zip(masks[:-1][::-1], values[:-1][::-1]):
        out = jnp.where(mask, value, out)
    return out


def lane_gather(x, index):
    return jnp.take_along_axis(x, index, axis=1, mode="promise_in_bounds")


def deal(parts, lane):
    low = [(lane & 3) == q for q in range(4)]
    block = [(lane >> 5) == v for v in range(4)]
    moved = []
    for d in range(4):
        merged = pick([low[(v + d) & 3] for v in range(4)], parts)
        moved.append(lane_gather(merged, 4 * (lane & 31) + (((lane >> 5) + d) & 3)))
    return [pick(block, [moved[(s - v) & 3] for v in range(4)]) for s in range(4)]


def undeal(planes, lane):
    low = [(lane & 3) == q for q in range(4)]
    block = [(lane >> 5) == v for v in range(4)]
    moved = []
    for d in range(4):
        merged = pick(block, [planes[(v + d) & 3] for v in range(4)])
        moved.append(lane_gather(merged, 32 * (((lane & 3) - d) & 3) + (lane >> 2)))
    return [pick(low, [moved[(q - v) & 3] for q in range(4)]) for v in range(4)]


def roll(x, shift, axis):
    shift = shift % x.shape[axis]
    return pltpu.roll(x, shift, axis) if shift else x


def kernel(split, *refs):
    ny, nzh, ncore, nzl, nx = (split[k] for k in ("y", "zh", "core", "zl", "x"))
    nrow, ncol = ny * nzh * ncore, nzl * nx
    inputs, refs = refs[:6], refs[6:]
    kept_ref, c_ref = refs[:2]
    (raw, rw_ref, dw_ref, diag_ref, inv_ref, lw_ref, uw_ref,
     s1h, s1u, s1d, sh, su, sd, landed,
     part, slots,
     in_sem, sx_sem, gx_sem, sr_sem, gr_sem) = refs[2:]

    got1 = landed.at[pl.ds(0, 51)]
    got = [landed.at[pl.ds(51 + 12 * j, 12)] for j in range(2)]
    row, col = lax.axis_index("row"), lax.axis_index("col")
    up, down = lax.rem(row + nrow - 1, nrow), lax.rem(row + 1, nrow)
    left, right = lax.rem(col + ncol - 1, ncol), lax.rem(col + 1, ncol)
    neighbours = [(up, left), (up, right), (down, left), (down, right), (up, col), (down, col), (row, left), (row, right)]

    y, zh, core = row // (nzh * ncore), lax.rem(row // ncore, nzh), lax.rem(row, ncore)
    zl, x = col // nx, lax.rem(col, nx)
    z = zh * nzl + zl

    def device(y, z, core, x):
        return ((y * nzh + z // nzl) * ncore + core, lax.rem(z, nzl) * nx + x)

    nz = nzh * nzl

    def ring(k, n):
        return min(k, n - k)

    stage_a = sorted(((ring(i, nx) + ring(k, nz), i, k) for i in range(nx) for k in range(nz) if i or k), reverse=True)
    stage_b = sorted(((ring(k, ny), k, i) for k in range(ny) for i in range(ncore) if i or k), reverse=True)
    hops_a = [far for far, _, _ in stage_a]
    stage_a = [device(y, lax.rem(z + k, nz), core, lax.rem(x + i, nx)) for _, i, k in stage_a]
    stage_b = [device(lax.rem(y + k, ny), z, lax.rem(core + i, ncore), x) for _, k, i in stage_b]

    farther = sum(far > 5 for far in hops_a)
    partners = stage_a[:farther] + neighbours + stage_a[farther:] + stage_b
    barrier = pltpu.get_barrier_semaphore()
    for who in partners[:farther + 8]:
        pl.semaphore_signal(barrier, inc=1, device_id=who, device_id_type=MESH)

    loads = [
        [pltpu.make_async_copy(src.at[:, 128 * v:128 * v + 128], raw.at[k, v], in_sem.at[k]) for v in range(4)]
        for k, src in enumerate(inputs)
    ]
    for k in (2, 3, 0, 1, 4, 5):
        for copy in loads[k]:
            copy.start()

    for who in partners[farther + 8:]:
        pl.semaphore_signal(barrier, inc=1, device_id=who, device_id_type=MESH)

    def finish(ref, sem):
        pltpu.make_async_copy(ref, ref, sem).wait()

    shape = (24, 128)
    lane, sub = iota(shape, 1), iota(shape, 0)
    lane8, sub8 = iota((8, 128), 1), iota((8, 128), 0)

    def load(k):
        finish(raw.at[k], in_sem.at[k])
        out = []
        for t in range(4):
            parts = [raw[k, v, pl.ds(t, 24, stride=4), :] for v in range(4)]
            out += deal(parts, lane)
        return out

    def pack_cols(planes, source, base, out=None):
        for t, plane in enumerate(planes):
            moved = roll(plane, base + t - source, 1)
            out = moved if out is None else jnp.where(lane == base + t, moved, out)
        return out

    def pack_rows(planes, source, base, out=None):
        for s, plane in enumerate(planes):
            tile = plane[8 * (source // 8):8 * (source // 8) + 8]
            moved = roll(tile, base + s - source % 8, 0)
            out = moved if out is None else jnp.where(sub8 == base + s, moved, out)
        return out

    rw = load(2)
    at_end = jnp.logical_and(lane == 127, col == ncol - 1)
    for t in range(4):
        rw[4 * t + 3] = jnp.where(at_end, 0.0, rw[4 * t + 3])
    dw = load(3)
    at_end = jnp.logical_and(sub == 23, row == nrow - 1)
    for s in range(4):
        dw[12 + s] = jnp.where(at_end, 0.0, dw[12 + s])
    fx = [a * b for a, b in zip(rw, load(0))]
    fy = [a * b for a, b in zip(dw, load(1))]
    anchor = load(4)
    prior = load(5)

    def behind(planes):
        return [jnp.where(lane == 0, 0.0, roll(planes[4 * t + 3], 1, 1)) for t in range(4)]

    def above(planes):
        return [jnp.where(sub == 0, 0.0, roll(planes[12 + s], 1, 0)) for s in range(4)]

    def spread(first, planes, step):
        if step == 1:
            return [first[k // 4] if k % 4 == 0 else planes[k - 1] for k in range(16)]
        return [first[k] if k < 4 else planes[k - 4] for k in range(16)]

    lw0, fl0, uw0, fu0 = behind(rw), behind(fx), above(dw), above(fy)
    lw, fl, uw, fu = spread(lw0, rw, 1), spread(fl0, fx, 1), spread(uw0, dw, 4), spread(fu0, fy, 4)
    diag = [anchor[k] + lw[k] + rw[k] + uw[k] + dw[k] for k in range(16)]
    resid = [anchor[k] * prior[k] - fx[k] - fy[k] + fl[k] + fu[k] for k in range(16)]

    def total(planes):
        while len(planes) > 1:
            planes = [a + b for a, b in zip(planes[::2], planes[1::2])]
        return planes[0]

    c_right, c_down = total(rw[3::4]), total(dw[12:])
    c_diag = total(anchor) + total(lw0) + c_right + total(uw0) + c_down
    c_resid, c_fx, c_fy = total(resid), total(fx[3::4]), total(fy[12:])

    def side_tile(coarse, planes=None, edge=None):
        h = coarse
        if planes is not None:
            h = pack_cols(planes[3::4], 127, 120, pack_cols(planes[0::4], 0, 4, h))
        if edge is not None:
            h = pack_cols(edge[3::4], 127, 116, h)
        return h

    h0, h1 = side_tile(c_right, diag, rw), side_tile(c_down, resid, fx)
    h2 = jnp.where(lane == 119, roll(c_fx, -8, 1), c_diag)
    h3 = jnp.where(
        jnp.logical_and(lane >= 4, lane < 8), roll(c_fy, 4, 1),
        jnp.where(jnp.logical_and(lane >= 120, lane < 124), roll(c_fy, -4, 1), c_resid),
    )
    for k, h in enumerate((h0, h1, h2, h3)):
        s1h[3 * k:3 * k + 3] = h.reshape(3, 8, 128)
    s1u[0] = pack_rows(diag[:4], 0, 4, c_right[:8])
    s1u[1] = pack_rows(resid[:4], 0, 4, c_down[:8])
    s1u[2] = jnp.where(sub8 < 4, c_diag[:8], roll(c_fx[:8], 4, 0))
    s1u[3] = pack_rows([rw[3], fx[3]], 0, 4, c_resid[:8])
    s1d[0] = pack_rows(diag[12:], 23, 0, c_right[16:])
    s1d[1] = pack_rows(resid[12:], 23, 0, c_down[16:])
    s1d[2] = jnp.where(sub8 >= 4, c_diag[16:], roll(c_fx[16:], 4, 0))
    s1d[3] = pack_rows([c_fy, rw[15], fx[15]], 23, 0, c_resid[16:])
    d4 = pack_rows(fy[12:], 23, 4, pack_rows(dw[12:], 23, 0))
    s1d[4] = d4

    def pack(coarse, planes, h_ref, u_ref, d_ref):
        h_ref[...] = side_tile(coarse, planes).reshape(3, 8, 128)
        u_ref[0] = pack_rows(planes[:4], 0, 4, coarse[:8])
        d_ref[0] = pack_rows(planes[12:], 23, 0, coarse[16:])

    def exchange(h, u, d, got, nu, nd, send, recv):
        nh = h.shape[0]
        plan = [(u, 1, (up, left)), (u, 2, (up, right)), (d, 4, (down, left)), (d, 5, (down, right))]
        plan += [(u, 0, (up, col)), (d, 3, (down, col))]
        plan = [
            (src, got.at[pl.ds(2 * nh + (nu * k if k < 3 else 3 * nu + nd * (k - 3)), nu if k < 3 else nd)], who)
            for src, k, who in plan
        ]
        plan += [(h, got.at[pl.ds(0, nh)], (row, left)), (h, got.at[pl.ds(nh, nh)], (row, right))]
        for src, dst, who in plan:
            pltpu.make_async_remote_copy(src, dst, send, recv, device_id=who, device_id_type=MESH).start()

    pl.semaphore_wait(barrier, len(partners))
    exchange(s1h, s1u, s1d, got1, 4, 5, sx_sem, gx_sem.at[0])
    for k in range(16):
        rw_ref[k] = rw[k]
        dw_ref[k] = dw[k]

    def assemble(own, h, v, fill=0.0):
        side = jnp.where(lane < 64, h[0], h[1])
        ring = jnp.where(jnp.logical_or(lane < 4, lane >= 124), side, fill)
        below = jnp.where(sub8 < 4, v[0], v[3])
        corner = jnp.where(
            lane8 < 4,
            jnp.where(sub8 < 4, v[1], v[4]),
            jnp.where(lane8 >= 124, jnp.where(sub8 < 4, v[2], v[5]), fill),
        )
        ends = jnp.where(sub8 < 4, v[3], v[0])
        return quad(own, ring, below, corner), side, ends

    def quad(own, ring, below, corner):
        return jnp.concatenate(
            [jnp.concatenate([own, ring], axis=1), jnp.concatenate([below, corner], axis=1)], axis=0
        )

    finish(got1, gx_sem.at[0])
    hs = [[got1[pl.ds(12 * k + 3 * f, 3)].reshape(shape) for k in range(2)] for f in range(4)]
    vs = [[got1[24 + 4 * k + f] for k in range(3)] + [got1[36 + 5 * k + f] for k in range(3)] for f in range(4)]
    from_up, from_up_right, from_up_left = (got1[36 + 5 * k + 4] for k in range(3))

    cr, diag_side, diag_ends = assemble(c_right, hs[0], vs[0])
    cd, side, ends = assemble(c_down, hs[1], vs[1])
    cdiag, _, _ = assemble(c_diag, hs[2], vs[2], 1.0)
    ext, _, _ = assemble(c_resid, hs[3], vs[3])

    lane_x, sub_x = iota((32, 256), 1), iota((32, 256), 0)
    first_col = (lane_x & 127) == 0
    first_row = jnp.logical_or(sub_x == 0, sub_x == 24)
    cdiag = cdiag + jnp.where(first_col, roll(cr, 1, 1), 0.0) + jnp.where(first_row, roll(cd, 1, 0), 0.0)
    across = quad(
        roll(hs[2][1], 9, 1),
        roll(c_fx, 1, 1),
        roll(roll(jnp.where(sub8 < 4, vs[2][5], vs[2][2]), 4, 0), 1, 1),
        roll(roll(jnp.where(sub8 < 4, vs[2][3], vs[2][0]), 4, 0), 1, 1),
    )
    ext = ext + jnp.where(first_col, across, 0.0)
    beyond = jnp.where(lane8 < 64, vs[3][4], vs[3][5])
    near = jnp.where(lane < 64, roll(hs[3][0], -4, 1), roll(hs[3][1], 4, 1))
    across = quad(
        jnp.broadcast_to(vs[3][3][0:1], shape),
        jnp.broadcast_to(beyond[0:1], shape),
        roll(c_fy[16:], 1, 0),
        roll(near[16:], 1, 0),
    )
    in_ring = jnp.logical_or(lane_x < 132, lane_x >= 252)
    ext = ext + jnp.where(jnp.logical_and(first_row, in_ring), across, 0.0)

    to_right = jnp.logical_and(lane >= 4, lane < 8)
    to_left = jnp.logical_and(lane >= 120, lane < 124)
    top_right = jnp.logical_and(sub == 0, lane == 4)
    top_left = jnp.logical_and(sub == 0, lane == 120)
    far_right, far_left = roll(from_up_right, 4, 1), roll(from_up_left, -7, 1)
    col_up, col_down = roll(vs[3][5], 1, 1), roll(vs[3][2], 1, 1)
    up_corner = jnp.logical_and(lane8 == 0, sub8 == 0)
    down_corner = jnp.logical_and(lane8 == 0, sub8 == 4)

    def complete(at_side, at_ends, edge, row_edge, n):
        at_side = at_side + jnp.where(to_right, roll(edge, 16, 1), 0.0)
        at_side = at_side + jnp.where(top_right, jnp.broadcast_to(far_right[4 * n:4 * n + 1], shape), 0.0)
        at_side = at_side + jnp.where(top_left, jnp.broadcast_to(far_left[4 * n + 3:4 * n + 4], shape), 0.0)
        at_ends = at_ends + jnp.where(sub8 >= 4, row_edge, 0.0)
        at_ends = at_ends + jnp.where(up_corner, jnp.broadcast_to(col_up[1 + n:2 + n], (8, 128)), 0.0)
        at_ends = at_ends + jnp.where(down_corner, jnp.broadcast_to(col_down[4 + n:5 + n], (8, 128)), 0.0)
        return at_side, at_ends

    diag_side, diag_ends = complete(diag_side, diag_ends, h0, roll(d4, 4, 0), 0)
    side, ends = complete(side, ends, h1, d4, 1)
    inv_side = 1.0 / jnp.where(jnp.logical_or(to_right, to_left), diag_side, 1.0)
    inv_ends = 1.0 / diag_ends

    for t in range(4):
        more = jnp.where(lane == 0, roll(hs[0][1], -(116 + t), 1), 0.0)
        lw0[t] = lw0[t] + more
        diag[4 * t] = diag[4 * t] + more
        resid[4 * t] = resid[4 * t] + jnp.where(lane == 0, roll(hs[1][1], -(116 + t), 1), 0.0)
    for s in range(4):
        more = jnp.where(sub == 0, jnp.broadcast_to(from_up[s:s + 1], shape), 0.0)
        uw0[s] = uw0[s] + more
        diag[s] = diag[s] + more
        resid[s] = resid[s] + jnp.where(sub == 0, jnp.broadcast_to(from_up[4 + s:5 + s], shape), 0.0)
    inv = [1.0 / d for d in diag]
    for k in range(16):
        diag_ref[k] = diag[k]
        inv_ref[k] = inv[k]
    for k in range(4):
        lw_ref[k] = lw0[k]
        uw_ref[k] = uw0[k]

    scale = OMEGA / cdiag
    a_right, a_left = scale * cr, scale * roll(cr, 1, 1)
    a_down, a_up = scale * cd, scale * roll(cd, 1, 0)

    def smooth(ext, side, ends):
        start = scale * ext
        level = start
        for turn in range(3):
            beside = a_left * roll(level, 1, 1) + a_right * roll(level, -1, 1)
            beside = beside + a_up * roll(level, 1, 0) + a_down * roll(level, -1, 0)
            level = (1.0 - OMEGA) * level + (start + beside)
        e_side, e_ends = level[:24, 128:], level[24:, :128]
        e_side = jnp.where(
            lane < 64, jnp.broadcast_to(e_side[:, 0:1], shape), jnp.broadcast_to(e_side[:, 127:128], shape)
        )
        e_ends = jnp.where(
            sub8 < 4, jnp.broadcast_to(e_ends[7:8], (8, 128)), jnp.broadcast_to(e_ends[0:1], (8, 128))
        )
        return level[:24, :128], inv_side * side + e_side, inv_ends * ends + e_ends

    def operate(v, side, ends, emit):
        west = [jnp.where(lane == 0, roll(side, -(120 + t), 1), roll(v[4 * t + 3], 1, 1)) for t in range(4)]
        east = [jnp.where(lane == 127, roll(side, 127 - (4 + t), 1), roll(v[4 * t], -1, 1)) for t in range(4)]
        north = [
            jnp.where(sub == 0, jnp.broadcast_to(ends[s:s + 1], shape), roll(v[12 + s], 1, 0)) for s in range(4)
        ]
        south = [
            jnp.where(sub == 23, jnp.broadcast_to(ends[4 + s:5 + s], shape), roll(v[s], -1, 0)) for s in range(4)
        ]
        for k in range(16):
            t, s = k // 4, k % 4
            beside = (lw_ref[t] * west[t]) if s == 0 else (rw_ref[k - 1] * v[k - 1])
            beside = beside + rw_ref[k] * (east[t] if s == 3 else v[k + 1])
            beside = beside + ((uw_ref[s] * north[s]) if t == 0 else (dw_ref[k - 4] * v[k - 4]))
            beside = beside + dw_ref[k] * (south[s] if t == 3 else v[k + 4])
            emit(k, diag_ref[k] * v[k] - beside)

    def dot(a, b):
        return total([a[k] * b[k] for k in range(16)])

    sums = {}
    news = ext, side, ends
    images, fields = [], []
    for j in range(3):
        if j:
            finish(got[j - 1], gx_sem.at[j])
            news = assemble(
                coarse, [got[j - 1][3 * k:3 * k + 3].reshape(shape) for k in range(2)], [got[j - 1][6 + k] for k in range(6)]
            )
        level, new_side, new_ends = smooth(*news)
        if j == 0:
            v = [inv_ref[k] * resid[k] + level for k in range(16)]
            side, ends = new_side, new_ends
        else:
            v = [inv_ref[k] * images[-1][k] + level - fields[-1][k] for k in range(16)]
            side, ends = new_side - side, new_ends - ends
        image = [None] * 16

        def emit(k, value):
            image[k] = value

        operate(v, side, ends, emit)
        fields.append(v)
        images.append(image)
        if j < 2:
            coarse = total(image)
            pack(coarse, image, sh.at[j], su.at[j], sd.at[j])
            exchange(sh.at[j], su.at[j], sd.at[j], got[j], 1, 1, sx_sem, gx_sem.at[j + 1])
        sums["g", j] = dot(resid, v)
        for i in range(j + 1):
            sums[i, j] = dot(images[i], v)

    order = [("g", 0), ("g", 1), ("g", 2), (0, 0), (0, 1), (0, 2), (1, 1), (1, 2), (2, 2)]
    sums_row = jnp.zeros((1, 128), F)
    lane1 = iota((1, 128), 1)
    for k, name in enumerate(order):
        x8 = sums[name]
        x8 = x8[:8] + x8[8:16] + x8[16:]
        for shift in (64, 32, 16, 8):
            x8 = x8 + roll(x8, shift, 1)
        one = jnp.sum(x8, axis=0, keepdims=True)
        sums_row = jnp.where((lane1 >> 3) == k, one, sums_row)

    def keep(n, planes):
        for t in range(4):
            for v, value in enumerate(undeal(planes[4 * t:4 * t + 4], lane)):
                kept_ref[n, v, pl.ds(t, 24, stride=4), :] = value

    base = 0
    for stage, others in enumerate((stage_a, stage_b)):
        part[stage] = sums_row
        for k, who in enumerate(others):
            pltpu.make_async_remote_copy(
                part.at[stage], slots.at[base + k], sr_sem, gr_sem.at[stage], device_id=who, device_id_type=MESH
            ).start()
        for n in range(4) if stage == 0 else range(4, 7):
            keep(n, resid if n == 0 else (fields[n - 1] if n < 4 else images[n - 4]))
        finish(slots.at[pl.ds(base, len(others))], gr_sem.at[stage])
        sums_row = total_any([sums_row] + [slots[base + k] for k in range(len(others))])
        base += len(others)

    for shift in (4, 2, 1):
        sums_row = sums_row + roll(sums_row, -shift, 1)
    value = {
        name: jnp.broadcast_to(sums_row[:, 8 * k:8 * k + 1], (1, 128)) for k, name in enumerate(order)
    }
    g0, g1, g2 = (value["g", j] for j in range(3))
    a00, a01, a02 = value[0, 0], value[0, 1], value[0, 2]
    l10, l20 = a01 / a00, a02 / a00
    d1, t12 = value[1, 1] - l10 * a01, value[1, 2] - l10 * a02
    l21 = t12 / d1
    d2 = value[2, 2] - l20 * a02 - l21 * t12
    y1 = g1 - l10 * g0
    y2 = g2 - l20 * g0 - l21 * y1
    c2 = y2 / d2
    c1 = y1 / d1 - l21 * c2
    c0 = g0 / a00 - l10 * c1 - l20 * c2
    for k, value in enumerate((c0, c1, c2)):
        c_ref[k] = jnp.broadcast_to(value, (8, 128))

    finish(landed, sx_sem)
    finish(slots, sr_sem)


def combine(kept_ref, c_ref, heights_ref, resid_ref, done, sem):
    c = [c_ref[k] for k in range(3)]
    for v in range(4):
        for i in range(0, kept_ref.shape[2], 8):
            r0, u0, u1, u2, w0, w1, w2 = (kept_ref[n, v, i:i + 8] for n in range(7))
            done[0, v, i:i + 8] = c[0] * u0 + c[1] * u1 + c[2] * u2
            done[1, v, i:i + 8] = r0 - (c[0] * w0 + c[1] * w1 + c[2] * w2)
        for n, out_ref in enumerate((heights_ref, resid_ref)):
            pltpu.make_async_copy(done.at[n, v], out_ref.at[:, 128 * v:128 * v + 128], sem).start()
    pltpu.make_async_copy(done, done, sem).wait()


def total_any(values):
    while len(values) > 1:
        rest = values[len(values) // 2 * 2:]
        values = [a + b for a, b in zip(values[::2], values[1::2])] + rest
    return values[0]


def solution(mesh, split=SPLIT):
    others = split["x"] * split["zh"] * split["zl"] + split["y"] * split["core"] - 2

    def step(*args):
        rows, cols = args[0].shape
        assert (rows, cols) == (96, 512)
        shapes = [(7, 4, rows, 128), (3, 8, 128)]
        dma = pltpu.SemaphoreType.DMA

        def vmem(*shape):
            return pltpu.VMEM(shape, F)

        args = [pltpu.with_memory_space_constraint(x, pltpu.HBM) for x in args]
        parts = pl.pallas_call(
            functools.partial(kernel, split),
            out_shape=[jax.ShapeDtypeStruct(shape, F) for shape in shapes],
            in_specs=[pl.BlockSpec(memory_space=pltpu.HBM)] * 6,
            out_specs=[pl.BlockSpec(memory_space=pltpu.VMEM)] * 2,
            scratch_shapes=[
                vmem(6, 4, rows, 128),
                vmem(16, 24, 128), vmem(16, 24, 128), vmem(16, 24, 128), vmem(16, 24, 128),
                vmem(4, 24, 128), vmem(4, 24, 128),
                vmem(12, 8, 128), vmem(4, 8, 128), vmem(5, 8, 128),
                vmem(2, 3, 8, 128), vmem(2, 1, 8, 128), vmem(2, 1, 8, 128), vmem(75, 8, 128),
                vmem(2, 1, 128), vmem(others, 1, 128),
                dma((6,)), dma(()), dma((3,)), dma(()), dma((2,)),
            ],
            compiler_params=pltpu.CompilerParams(
                collective_id=0, has_side_effects=True, vmem_limit_bytes=12 * 2**20
            ),
        )(*args)
        return tuple(pl.pallas_call(
            combine,
            out_shape=[jax.ShapeDtypeStruct((rows, cols), F)] * 2,
            in_specs=[pl.BlockSpec(memory_space=pltpu.VMEM)] * 2,
            out_specs=[pl.BlockSpec(memory_space=pltpu.HBM)] * 2,
            scratch_shapes=[vmem(2, 4, rows, 128), dma(())],
            compiler_params=pltpu.CompilerParams(vmem_limit_bytes=12 * 2**20),
        )(*parts))

    return jax.shard_map(
        step,
        mesh=mesh,
        in_specs=(P("row", "col"),) * 6,
        out_specs=(P("row", "col"),) * 2,
        check_vma=False,
    )
```

```python
import functools

import jax
import jax.numpy as jnp
from jax import lax
from jax.experimental import pallas as pl
from jax.experimental.pallas import tpu as pltpu
from jax.sharding import PartitionSpec as P

MESH = pl.DeviceIdType.MESH
F = jnp.float32
OMEGA = 2.0 / 3.0

SPLIT = dict(y=8, zh=4, core=2, zl=2, x=4)


def iota(shape, dim):
    return lax.broadcasted_iota(jnp.int32, shape, dim)


def pick(masks, values):
    out = values[-1]
    for mask, value in zip(masks[:-1][::-1], values[:-1][::-1]):
        out = jnp.where(mask, value, out)
    return out


def lane_gather(x, index):
    return jnp.take_along_axis(x, index, axis=1, mode="promise_in_bounds")


def deal(parts, lane):
    low = [(lane & 3) == q for q in range(4)]
    block = [(lane >> 5) == v for v in range(4)]
    moved = []
    for d in range(4):
        merged = pick([low[(v + d) & 3] for v in range(4)], parts)
        moved.append(lane_gather(merged, 4 * (lane & 31) + (((lane >> 5) + d) & 3)))
    return [pick(block, [moved[(s - v) & 3] for v in range(4)]) for s in range(4)]


def undeal(planes, lane):
    low = [(lane & 3) == q for q in range(4)]
    block = [(lane >> 5) == v for v in range(4)]
    moved = []
    for d in range(4):
        merged = pick(block, [planes[(v + d) & 3] for v in range(4)])
        moved.append(lane_gather(merged, 32 * (((lane & 3) - d) & 3) + (lane >> 2)))
    return [pick(low, [moved[(q - v) & 3] for q in range(4)]) for v in range(4)]


def roll(x, shift, axis):
    shift = shift % x.shape[axis]
    return pltpu.roll(x, shift, axis) if shift else x


def kernel(split, *refs):
    ny, nzh, ncore, nzl, nx = (split[k] for k in ("y", "zh", "core", "zl", "x"))
    nrow, ncol = ny * nzh * ncore, nzl * nx
    inputs, refs = refs[:6], refs[6:]
    kept_ref, c_ref = refs[:2]
    (raw, rw_ref, dw_ref, diag_ref, inv_ref, lw_ref, uw_ref, u_ref, w_ref, sums_ref, coarse_ref,
     s1h, s1u, s1d, sh, su, sd, landed,
     part, slots,
     in_sem, sx_sem, gx_sem, sr_sem, gr_sem) = refs[2:]

    got1 = landed.at[pl.ds(0, 51)]
    got = [landed.at[pl.ds(51 + 12 * j, 12)] for j in range(2)]
    row, col = lax.axis_index("row"), lax.axis_index("col")

    def wrap(k, n):
        return jnp.where(k >= n, k - n, k)

    up, down = wrap(row + nrow - 1, nrow), wrap(row + 1, nrow)
    left, right = wrap(col + ncol - 1, ncol), wrap(col + 1, ncol)
    neighbours = [(up, left), (up, right), (down, left), (down, right), (up, col), (down, col), (row, left), (row, right)]

    half = lax.div(row, jnp.int32(ncore))
    y, core = lax.div(row, jnp.int32(nzh * ncore)), row - half * ncore
    zh, zl = half - y * nzh, lax.div(col, jnp.int32(nx))
    x = col - zl * nx
    z = zh * nzl + zl

    def device(y, z, core, x):
        high = lax.div(z, jnp.int32(nzl))
        return ((y * nzh + high) * ncore + core, (z - high * nzl) * nx + x)

    nz = nzh * nzl

    def ring(k, n):
        return min(k, n - k)

    stage_a = sorted(((ring(i, nx) + ring(k, nz), i, k) for i in range(nx) for k in range(nz) if i or k), reverse=True)
    stage_b = sorted(((ring(k, ny), k, i) for k in range(ny) for i in range(ncore) if i or k), reverse=True)
    hops_a = [far for far, _, _ in stage_a]
    stage_a = [device(y, wrap(z + k, nz), core, wrap(x + i, nx)) for _, i, k in stage_a]
    stage_b = [device(wrap(y + k, ny), z, wrap(core + i, ncore), x) for _, k, i in stage_b]

    farther = sum(far > 5 for far in hops_a)
    partners = stage_a[:farther] + neighbours + stage_a[farther:] + stage_b
    barrier = pltpu.get_barrier_semaphore()
    for who in partners[:farther + 8]:
        pl.semaphore_signal(barrier, inc=1, device_id=who, device_id_type=MESH)

    loads = [
        [pltpu.make_async_copy(src.at[:, 128 * v:128 * v + 128], raw.at[k, v], in_sem.at[k]) for v in range(4)]
        for k, src in enumerate(inputs)
    ]
    for k in (2, 3, 0, 1, 4, 5):
        for copy in loads[k]:
            copy.start()

    for who in partners[farther + 8:]:
        pl.semaphore_signal(barrier, inc=1, device_id=who, device_id_type=MESH)

    def finish(ref, sem):
        pltpu.make_async_copy(ref, ref, sem).wait()

    shape = (24, 128)
    lane, sub = iota(shape, 1), iota(shape, 0)
    lane8, sub8 = iota((8, 128), 1), iota((8, 128), 0)

    def load(k):
        finish(raw.at[k], in_sem.at[k])
        out = []
        for t in range(4):
            parts = [raw[k, v, pl.ds(t, 24, stride=4), :] for v in range(4)]
            out += deal(parts, lane)
        return out

    def pack_cols(planes, source, base, out=None):
        for t, plane in enumerate(planes):
            moved = roll(plane, base + t - source, 1)
            out = moved if out is None else jnp.where(lane == base + t, moved, out)
        return out

    def pack_rows(planes, source, base, out=None):
        for s, plane in enumerate(planes):
            tile = plane[8 * (source // 8):8 * (source // 8) + 8]
            moved = roll(tile, base + s - source % 8, 0)
            out = moved if out is None else jnp.where(sub8 == base + s, moved, out)
        return out

    rw = load(2)
    at_end = jnp.logical_and(lane == 127, col == ncol - 1)
    for t in range(4):
        rw[4 * t + 3] = jnp.where(at_end, 0.0, rw[4 * t + 3])
    dw = load(3)
    at_end = jnp.logical_and(sub == 23, row == nrow - 1)
    for s in range(4):
        dw[12 + s] = jnp.where(at_end, 0.0, dw[12 + s])
    fx = [a * b for a, b in zip(rw, load(0))]
    fy = [a * b for a, b in zip(dw, load(1))]
    anchor = load(4)
    prior = load(5)

    def behind(planes):
        return [jnp.where(lane == 0, 0.0, roll(planes[4 * t + 3], 1, 1)) for t in range(4)]

    def above(planes):
        return [jnp.where(sub == 0, 0.0, roll(planes[12 + s], 1, 0)) for s in range(4)]

    def spread(first, planes, step):
        if step == 1:
            return [first[k // 4] if k % 4 == 0 else planes[k - 1] for k in range(16)]
        return [first[k] if k < 4 else planes[k - 4] for k in range(16)]

    lw0, fl0, uw0, fu0 = behind(rw), behind(fx), above(dw), above(fy)
    lw, fl, uw, fu = spread(lw0, rw, 1), spread(fl0, fx, 1), spread(uw0, dw, 4), spread(fu0, fy, 4)
    diag = [anchor[k] + lw[k] + rw[k] + uw[k] + dw[k] for k in range(16)]
    resid = [anchor[k] * prior[k] - fx[k] - fy[k] + fl[k] + fu[k] for k in range(16)]

    def total(planes):
        while len(planes) > 1:
            planes = [a + b for a, b in zip(planes[::2], planes[1::2])]
        return planes[0]

    c_right, c_down = total(rw[3::4]), total(dw[12:])
    c_diag = total(anchor) + total(lw0) + c_right + total(uw0) + c_down
    c_resid, c_fx, c_fy = total(resid), total(fx[3::4]), total(fy[12:])

    def side_tile(coarse, planes=None, edge=None):
        h = coarse
        if planes is not None:
            h = pack_cols(planes[3::4], 127, 120, pack_cols(planes[0::4], 0, 4, h))
        if edge is not None:
            h = pack_cols(edge[3::4], 127, 116, h)
        return h

    h0, h1 = side_tile(c_right, diag, rw), side_tile(c_down, resid, fx)
    h2 = jnp.where(lane == 119, roll(c_fx, -8, 1), c_diag)
    h3 = jnp.where(
        jnp.logical_and(lane >= 4, lane < 8), roll(c_fy, 4, 1),
        jnp.where(jnp.logical_and(lane >= 120, lane < 124), roll(c_fy, -4, 1), c_resid),
    )
    for k, h in enumerate((h0, h1, h2, h3)):
        s1h[3 * k:3 * k + 3] = h.reshape(3, 8, 128)
    s1u[0] = pack_rows(diag[:4], 0, 4, c_right[:8])
    s1u[1] = pack_rows(resid[:4], 0, 4, c_down[:8])
    s1u[2] = jnp.where(sub8 < 4, c_diag[:8], roll(c_fx[:8], 4, 0))
    s1u[3] = pack_rows([rw[3], fx[3]], 0, 4, c_resid[:8])
    s1d[0] = pack_rows(diag[12:], 23, 0, c_right[16:])
    s1d[1] = pack_rows(resid[12:], 23, 0, c_down[16:])
    s1d[2] = jnp.where(sub8 >= 4, c_diag[16:], roll(c_fx[16:], 4, 0))
    s1d[3] = pack_rows([c_fy, rw[15], fx[15]], 23, 0, c_resid[16:])
    d4 = pack_rows(fy[12:], 23, 4, pack_rows(dw[12:], 23, 0))
    s1d[4] = d4

    def pack(coarse, planes, h_ref, u_ref, d_ref):
        h_ref[...] = side_tile(coarse, planes).reshape(3, 8, 128)
        u_ref[0] = pack_rows(planes[:4], 0, 4, coarse[:8])
        d_ref[0] = pack_rows(planes[12:], 23, 0, coarse[16:])

    def exchange(h, u, d, got, nu, nd, send, recv):
        nh = h.shape[0]
        plan = [(u, 1, (up, left)), (u, 2, (up, right)), (d, 4, (down, left)), (d, 5, (down, right))]
        plan += [(u, 0, (up, col)), (d, 3, (down, col))]
        plan = [
            (src, got.at[pl.ds(2 * nh + (nu * k if k < 3 else 3 * nu + nd * (k - 3)), nu if k < 3 else nd)], who)
            for src, k, who in plan
        ]
        plan += [(h, got.at[pl.ds(0, nh)], (row, left)), (h, got.at[pl.ds(nh, nh)], (row, right))]
        for src, dst, who in plan:
            pltpu.make_async_remote_copy(src, dst, send, recv, device_id=who, device_id_type=MESH).start()

    pl.semaphore_wait(barrier, len(partners))
    exchange(s1h, s1u, s1d, got1, 4, 5, sx_sem, gx_sem.at[0])
    inner = [k for k in range(16) if k >= 4 and k % 4]

    @pl.when(row >= 0)
    def _():
        for k in range(16):
            rw_ref[k] = rw[k]
            dw_ref[k] = dw[k]
        for k in inner:
            diag_ref[k] = diag[k]
            inv_ref[k] = 1.0 / diag[k]

    def assemble(own, h, v, fill=0.0):
        side = jnp.where(lane < 64, h[0], h[1])
        ring = jnp.where(jnp.logical_or(lane < 4, lane >= 124), side, fill)
        below = jnp.where(sub8 < 4, v[0], v[3])
        corner = jnp.where(
            lane8 < 4,
            jnp.where(sub8 < 4, v[1], v[4]),
            jnp.where(lane8 >= 124, jnp.where(sub8 < 4, v[2], v[5]), fill),
        )
        ends = jnp.where(sub8 < 4, v[3], v[0])
        return quad(own, ring, below, corner), side, ends

    def quad(own, ring, below, corner):
        return jnp.concatenate(
            [jnp.concatenate([own, ring], axis=1), jnp.concatenate([below, corner], axis=1)], axis=0
        )

    finish(got1, gx_sem.at[0])
    hs = [[got1[pl.ds(12 * k + 3 * f, 3)].reshape(shape) for k in range(2)] for f in range(4)]
    vs = [[got1[24 + 4 * k + f] for k in range(3)] + [got1[36 + 5 * k + f] for k in range(3)] for f in range(4)]
    from_up, from_up_right, from_up_left = (got1[36 + 5 * k + 4] for k in range(3))

    cr, diag_side, diag_ends = assemble(c_right, hs[0], vs[0])
    cd, side, ends = assemble(c_down, hs[1], vs[1])
    cdiag, _, _ = assemble(c_diag, hs[2], vs[2], 1.0)
    ext, _, _ = assemble(c_resid, hs[3], vs[3])

    lane_x, sub_x = iota((32, 256), 1), iota((32, 256), 0)
    first_col = (lane_x & 127) == 0
    first_row = jnp.logical_or(sub_x == 0, sub_x == 24)
    cdiag = cdiag + jnp.where(first_col, roll(cr, 1, 1), 0.0) + jnp.where(first_row, roll(cd, 1, 0), 0.0)
    across = quad(
        roll(hs[2][1], 9, 1),
        roll(c_fx, 1, 1),
        roll(roll(jnp.where(sub8 < 4, vs[2][5], vs[2][2]), 4, 0), 1, 1),
        roll(roll(jnp.where(sub8 < 4, vs[2][3], vs[2][0]), 4, 0), 1, 1),
    )
    ext = ext + jnp.where(first_col, across, 0.0)
    beyond = jnp.where(lane8 < 64, vs[3][4], vs[3][5])
    near = jnp.where(lane < 64, roll(hs[3][0], -4, 1), roll(hs[3][1], 4, 1))
    across = quad(
        jnp.broadcast_to(vs[3][3][0:1], shape),
        jnp.broadcast_to(beyond[0:1], shape),
        roll(c_fy[16:], 1, 0),
        roll(near[16:], 1, 0),
    )
    in_ring = jnp.logical_or(lane_x < 132, lane_x >= 252)
    ext = ext + jnp.where(jnp.logical_and(first_row, in_ring), across, 0.0)

    to_right = jnp.logical_and(lane >= 4, lane < 8)
    to_left = jnp.logical_and(lane >= 120, lane < 124)
    top_right = jnp.logical_and(sub == 0, lane == 4)
    top_left = jnp.logical_and(sub == 0, lane == 120)
    far_right, far_left = roll(from_up_right, 4, 1), roll(from_up_left, -7, 1)
    col_up, col_down = roll(vs[3][5], 1, 1), roll(vs[3][2], 1, 1)
    up_corner = jnp.logical_and(lane8 == 0, sub8 == 0)
    down_corner = jnp.logical_and(lane8 == 0, sub8 == 4)

    def complete(at_side, at_ends, edge, row_edge, n):
        at_side = at_side + jnp.where(to_right, roll(edge, 16, 1), 0.0)
        at_side = at_side + jnp.where(top_right, jnp.broadcast_to(far_right[4 * n:4 * n + 1], shape), 0.0)
        at_side = at_side + jnp.where(top_left, jnp.broadcast_to(far_left[4 * n + 3:4 * n + 4], shape), 0.0)
        at_ends = at_ends + jnp.where(sub8 >= 4, row_edge, 0.0)
        at_ends = at_ends + jnp.where(up_corner, jnp.broadcast_to(col_up[1 + n:2 + n], (8, 128)), 0.0)
        at_ends = at_ends + jnp.where(down_corner, jnp.broadcast_to(col_down[4 + n:5 + n], (8, 128)), 0.0)
        return at_side, at_ends

    diag_side, diag_ends = complete(diag_side, diag_ends, h0, roll(d4, 4, 0), 0)
    side, ends = complete(side, ends, h1, d4, 1)
    inv_side = 1.0 / jnp.where(jnp.logical_or(to_right, to_left), diag_side, 1.0)
    inv_ends = 1.0 / diag_ends

    for t in range(4):
        more = jnp.where(lane == 0, roll(hs[0][1], -(116 + t), 1), 0.0)
        lw0[t] = lw0[t] + more
        diag[4 * t] = diag[4 * t] + more
        resid[4 * t] = resid[4 * t] + jnp.where(lane == 0, roll(hs[1][1], -(116 + t), 1), 0.0)
    for s in range(4):
        more = jnp.where(sub == 0, jnp.broadcast_to(from_up[s:s + 1], shape), 0.0)
        uw0[s] = uw0[s] + more
        diag[s] = diag[s] + more
        resid[s] = resid[s] + jnp.where(sub == 0, jnp.broadcast_to(from_up[4 + s:5 + s], shape), 0.0)
    for k in range(16):
        if k not in inner:
            diag_ref[k] = diag[k]
            inv_ref[k] = 1.0 / diag[k]
    for k in range(4):
        lw_ref[k] = lw0[k]
        uw_ref[k] = uw0[k]

    scale = OMEGA / cdiag
    a_right, a_left = scale * cr, scale * roll(cr, 1, 1)
    a_down, a_up = scale * cd, scale * roll(cd, 1, 0)

    def smooth(ext, side, ends):
        start = scale * ext
        level = start
        for turn in range(3):
            beside = a_left * roll(level, 1, 1) + a_right * roll(level, -1, 1)
            beside = beside + a_up * roll(level, 1, 0) + a_down * roll(level, -1, 0)
            level = (1.0 - OMEGA) * level + (start + beside)
        e_side, e_ends = level[:24, 128:], level[24:, :128]
        e_side = jnp.where(
            lane < 64, jnp.broadcast_to(e_side[:, 0:1], shape), jnp.broadcast_to(e_side[:, 127:128], shape)
        )
        e_ends = jnp.where(
            sub8 < 4, jnp.broadcast_to(e_ends[7:8], (8, 128)), jnp.broadcast_to(e_ends[0:1], (8, 128))
        )
        return level, inv_side * side + e_side, inv_ends * ends + e_ends

    def borders(side, ends):
        west = [jnp.where(lane == 0, roll(side, -(120 + t), 1), 0.0) for t in range(4)]
        east = [jnp.where(lane == 127, roll(side, 127 - (4 + t), 1), 0.0) for t in range(4)]
        north = [jnp.where(sub == 0, jnp.broadcast_to(ends[s:s + 1], shape), 0.0) for s in range(4)]
        south = [jnp.where(sub == 23, jnp.broadcast_to(ends[4 + s:5 + s], shape), 0.0) for s in range(4)]
        return west, east, north, south

    def operate(v, around=None):
        west = [jnp.where(lane == 0, 0.0 if around is None else around[0][t], roll(v[4 * t + 3], 1, 1)) for t in range(4)]
        east = [jnp.where(lane == 127, 0.0 if around is None else around[1][t], roll(v[4 * t], -1, 1)) for t in range(4)]
        north = [jnp.where(sub == 0, 0.0 if around is None else around[2][s], roll(v[12 + s], 1, 0)) for s in range(4)]
        south = [jnp.where(sub == 23, 0.0 if around is None else around[3][s], roll(v[s], -1, 0)) for s in range(4)]
        image = []
        for k in range(16):
            t, s = k // 4, k % 4
            beside = (lw_ref[t] * west[t]) if s == 0 else (rw_ref[k - 1] * v[k - 1])
            beside = beside + rw_ref[k] * (east[t] if s == 3 else v[k + 1])
            beside = beside + ((uw_ref[s] * north[s]) if t == 0 else (dw_ref[k - 4] * v[k - 4]))
            beside = beside + dw_ref[k] * (south[s] if t == 3 else v[k + 4])
            image.append(diag_ref[k] * v[k] - beside)
        return image

    def dot(a, b):
        return total([a[k] * b[k] for k in range(16)])

    def fold(x):
        return x[:8] + x[8:16] + x[16:]

    order = [("g", 0), ("g", 1), ("g", 2), (0, 0), (0, 1), (0, 2), (1, 1), (1, 2), (2, 2)]
    news = ext, side, ends
    coarses, images = [ext[:24, :128]], [resid]
    for j in range(2):
        if j:
            finish(got[j - 1], gx_sem.at[j])
            news = assemble(
                coarses[j], [got[j - 1][3 * k:3 * k + 3].reshape(shape) for k in range(2)], [got[j - 1][6 + k] for k in range(6)]
            )
        level, new_side, new_ends = smooth(*news)
        own = level[:24, :128]
        if j == 0:
            v = [inv_ref[k] * resid[k] + own for k in range(16)]
            side, ends = new_side, new_ends
        else:
            v = [inv_ref[k] * images[j][k] + own - u_ref[0, k] for k in range(16)]
            side, ends = new_side - side, new_ends - ends
        image = operate(v, borders(side, ends))
        images.append(image)
        coarses.append(total(image))
        pack(coarses[-1], image, sh.at[j], su.at[j], sd.at[j])
        exchange(sh.at[j], su.at[j], sd.at[j], got[j], 1, 1, sx_sem, gx_sem.at[j + 1])
        for k in range(16):
            u_ref[j, k] = v[k]
            w_ref[j, k] = image[k]

        @pl.when(row >= 0)
        def _():
            v = [u_ref[j, k] for k in range(16)]
            sums_ref[order.index(("g", j))] = fold(dot(resid, v))
            for i in range(j + 1):
                sums_ref[order.index((i, j))] = fold(dot([w_ref[i, k] for k in range(16)], v))
            if j == 1:
                last = [w_ref[1, k] for k in range(16)]
                p = [inv_ref[k] * last[k] - v[k] for k in range(16)]
                image = operate(p)
                for k in range(16):
                    u_ref[2, k] = p[k]
                sums_ref[2] = fold(dot(resid, p))
                sums_ref[5] = fold(dot([w_ref[0, k] for k in range(16)], p))
                sums_ref[7] = fold(dot(last, p))
                sums_ref[8] = fold(dot(image, p))
                coarse_ref[...] = total(image)

    finish(got[1], gx_sem.at[2])
    ext, new_side, new_ends = assemble(
        coarses[2], [got[1][3 * k:3 * k + 3].reshape(shape) for k in range(2)], [got[1][6 + k] for k in range(6)]
    )
    p_side, p_ends = inv_side * new_side - side, inv_ends * new_ends - ends
    level, new_side, new_ends = smooth(ext, new_side, new_ends)
    side, ends = new_side - side, new_ends - ends
    own = level[:24, :128]
    beside = cr * roll(level, -1, 1) + roll(cr * level, 1, 1) + cd * roll(level, -1, 0) + roll(cd * level, 1, 0)
    c_image = (cdiag * level - beside)[:24, :128]
    cross, power = [], []
    west, east, north, south = borders(p_side, p_ends)
    for q in range(4):
        for weight, beyond, k in (
            (lw_ref[q], west[q], 4 * q), (rw_ref[4 * q + 3], east[q], 4 * q + 3),
            (uw_ref[q], north[q], q), (dw_ref[12 + q], south[q], 12 + q),
        ):
            flow = weight * beyond
            cross.append(flow)
            power.append(flow * u_ref[2, k])
    p_image = coarse_ref[...] - total(cross)
    sums = {name: sums_ref[k] for k, name in enumerate(order)}
    sums["g", 2] = sums["g", 2] + fold(coarses[0] * own)
    sums[0, 2] = sums[0, 2] + fold(coarses[1] * own)
    sums[1, 2] = sums[1, 2] + fold(coarses[2] * own)
    sums[2, 2] = sums[2, 2] + fold((c_image + 2.0 * p_image) * own - total(power))

    sums_row = jnp.zeros((1, 128), F)
    lane1 = iota((1, 128), 1)
    for k, name in enumerate(order):
        x8 = sums[name]
        for shift in (64, 32, 16, 8):
            x8 = x8 + roll(x8, shift, 1)
        one = jnp.sum(x8, axis=0, keepdims=True)
        sums_row = jnp.where((lane1 >> 3) == k, one, sums_row)

    def keep(n, planes):
        for t in range(4):
            for v, value in enumerate(undeal(planes[4 * t:4 * t + 4], lane)):
                kept_ref[n, v, pl.ds(t, 24, stride=4), :] = value

    base = 0
    for stage, others in enumerate((stage_a, stage_b)):
        part[stage] = sums_row
        for k, who in enumerate(others):
            pltpu.make_async_remote_copy(
                part.at[stage], slots.at[base + k], sr_sem, gr_sem.at[stage], device_id=who, device_id_type=MESH
            ).start()

        @pl.when(row >= 0)
        def _():
            if stage == 0:
                v = [u_ref[2, k] + own for k in range(16)]
                keep(3, v)
                keep(6, operate(v, borders(side, ends)))
            else:
                keep(0, resid)
                for j in range(2):
                    keep(1 + j, [u_ref[j, k] for k in range(16)])
                    keep(4 + j, [w_ref[j, k] for k in range(16)])

        finish(slots.at[pl.ds(base, len(others))], gr_sem.at[stage])
        sums_row = total_any([sums_row] + [slots[base + k] for k in range(len(others))])
        base += len(others)

    for shift in (4, 2, 1):
        sums_row = sums_row + roll(sums_row, -shift, 1)
    value = {
        name: jnp.broadcast_to(sums_row[:, 8 * k:8 * k + 1], (1, 128)) for k, name in enumerate(order)
    }
    g0, g1, g2 = (value["g", j] for j in range(3))
    a00, a01, a02 = value[0, 0], value[0, 1], value[0, 2]
    l10, l20 = a01 / a00, a02 / a00
    d1, t12 = value[1, 1] - l10 * a01, value[1, 2] - l10 * a02
    l21 = t12 / d1
    d2 = value[2, 2] - l20 * a02 - l21 * t12
    y1 = g1 - l10 * g0
    y2 = g2 - l20 * g0 - l21 * y1
    c2 = y2 / d2
    c1 = y1 / d1 - l21 * c2
    c0 = g0 / a00 - l10 * c1 - l20 * c2
    for k, value in enumerate((c0, c1, c2)):
        c_ref[k] = jnp.broadcast_to(value, (8, 128))

    finish(landed, sx_sem)
    finish(slots, sr_sem)


def combine(kept_ref, c_ref, heights_ref, resid_ref, done, sem):
    c = [c_ref[k] for k in range(3)]
    for v in range(4):
        for i in range(0, kept_ref.shape[2], 8):
            r0, u0, u1, u2, w0, w1, w2 = (kept_ref[n, v, i:i + 8] for n in range(7))
            done[0, v, i:i + 8] = c[0] * u0 + c[1] * u1 + c[2] * u2
            done[1, v, i:i + 8] = r0 - (c[0] * w0 + c[1] * w1 + c[2] * w2)
        for n, out_ref in enumerate((heights_ref, resid_ref)):
            pltpu.make_async_copy(done.at[n, v], out_ref.at[:, 128 * v:128 * v + 128], sem).start()
    pltpu.make_async_copy(done, done, sem).wait()


def total_any(values):
    while len(values) > 1:
        rest = values[len(values) // 2 * 2:]
        values = [a + b for a, b in zip(values[::2], values[1::2])] + rest
    return values[0]


def solution(mesh, split=SPLIT):
    others = split["x"] * split["zh"] * split["zl"] + split["y"] * split["core"] - 2

    def step(*args):
        rows, cols = args[0].shape
        assert (rows, cols) == (96, 512)
        shapes = [(7, 4, rows, 128), (3, 8, 128)]
        dma = pltpu.SemaphoreType.DMA

        def vmem(*shape):
            return pltpu.VMEM(shape, F)

        args = [pltpu.with_memory_space_constraint(x, pltpu.HBM) for x in args]
        parts = pl.pallas_call(
            functools.partial(kernel, split),
            out_shape=[jax.ShapeDtypeStruct(shape, F) for shape in shapes],
            in_specs=[pl.BlockSpec(memory_space=pltpu.HBM)] * 6,
            out_specs=[pl.BlockSpec(memory_space=pltpu.VMEM)] * 2,
            scratch_shapes=[
                vmem(6, 4, rows, 128),
                vmem(16, 24, 128), vmem(16, 24, 128), vmem(16, 24, 128), vmem(16, 24, 128),
                vmem(4, 24, 128), vmem(4, 24, 128),
                vmem(3, 16, 24, 128), vmem(2, 16, 24, 128), vmem(9, 8, 128), vmem(24, 128),
                vmem(12, 8, 128), vmem(4, 8, 128), vmem(5, 8, 128),
                vmem(2, 3, 8, 128), vmem(2, 1, 8, 128), vmem(2, 1, 8, 128), vmem(75, 8, 128),
                vmem(2, 1, 128), vmem(others, 1, 128),
                dma((6,)), dma(()), dma((3,)), dma(()), dma((2,)),
            ],
            compiler_params=pltpu.CompilerParams(
                collective_id=0, has_side_effects=True, vmem_limit_bytes=12 * 2**20
            ),
        )(*args)
        return tuple(pl.pallas_call(
            combine,
            out_shape=[jax.ShapeDtypeStruct((rows, cols), F)] * 2,
            in_specs=[pl.BlockSpec(memory_space=pltpu.VMEM)] * 2,
            out_specs=[pl.BlockSpec(memory_space=pltpu.HBM)] * 2,
            scratch_shapes=[vmem(2, 4, rows, 128), dma(())],
            compiler_params=pltpu.CompilerParams(vmem_limit_bytes=12 * 2**20),
        )(*parts))

    return jax.shard_map(
        step,
        mesh=mesh,
        in_specs=(P("row", "col"),) * 6,
        out_specs=(P("row", "col"),) * 2,
        check_vma=False,
    )
```

```python
import functools

import jax
import jax.numpy as jnp
from jax import lax
from jax.experimental import pallas as pl
from jax.experimental.pallas import tpu as pltpu
from jax.sharding import PartitionSpec as P

MESH = pl.DeviceIdType.MESH
F = jnp.float32
OMEGA = 2.0 / 3.0

SPLIT = dict(y=8, zh=4, core=2, zl=2, x=4)


def iota(shape, dim):
    return lax.broadcasted_iota(jnp.int32, shape, dim)


def pick(masks, values):
    out = values[-1]
    for mask, value in zip(masks[:-1][::-1], values[:-1][::-1]):
        out = jnp.where(mask, value, out)
    return out


def lane_gather(x, index):
    return jnp.take_along_axis(x, index, axis=1, mode="promise_in_bounds")


def deal(parts, lane):
    low = [(lane & 3) == q for q in range(4)]
    block = [(lane >> 5) == v for v in range(4)]
    moved = []
    for d in range(4):
        merged = pick([low[(v + d) & 3] for v in range(4)], parts)
        moved.append(lane_gather(merged, 4 * (lane & 31) + (((lane >> 5) + d) & 3)))
    return [pick(block, [moved[(s - v) & 3] for v in range(4)]) for s in range(4)]


def undeal(planes, lane):
    low = [(lane & 3) == q for q in range(4)]
    block = [(lane >> 5) == v for v in range(4)]
    moved = []
    for d in range(4):
        merged = pick(block, [planes[(v + d) & 3] for v in range(4)])
        moved.append(lane_gather(merged, 32 * (((lane & 3) - d) & 3) + (lane >> 2)))
    return [pick(low, [moved[(q - v) & 3] for q in range(4)]) for v in range(4)]


def roll(x, shift, axis):
    shift = shift % x.shape[axis]
    return pltpu.roll(x, shift, axis) if shift else x


def kernel(split, *refs):
    ny, nzh, ncore, nzl, nx = (split[k] for k in ("y", "zh", "core", "zl", "x"))
    nrow, ncol = ny * nzh * ncore, nzl * nx
    inputs, refs = refs[:6], refs[6:]
    kept_ref, c_ref = refs[:2]
    (raw, rw_ref, dw_ref, diag_ref, inv_ref, lw_ref, uw_ref, u_ref, w_ref, sums_ref, coarse_ref,
     s1h, s1u, s1d, sh, su, sd, landed,
     part, slots,
     in_sem, sx_sem, gx_sem, sr_sem, gr_sem) = refs[2:]

    got1 = landed.at[pl.ds(0, 51)]
    got = [landed.at[pl.ds(51 + 12 * j, 12)] for j in range(2)]
    row, col = lax.axis_index("row"), lax.axis_index("col")

    def wrap(k, n):
        return jnp.where(k >= n, k - n, k)

    up, down = wrap(row + nrow - 1, nrow), wrap(row + 1, nrow)
    left, right = wrap(col + ncol - 1, ncol), wrap(col + 1, ncol)
    neighbours = [(up, left), (up, right), (down, left), (down, right), (up, col), (down, col), (row, left), (row, right)]

    half = lax.div(row, jnp.int32(ncore))
    y, core = lax.div(row, jnp.int32(nzh * ncore)), row - half * ncore
    zh, zl = half - y * nzh, lax.div(col, jnp.int32(nx))
    x = col - zl * nx
    z = zh * nzl + zl

    def device(y, z, core, x):
        high = lax.div(z, jnp.int32(nzl))
        return ((y * nzh + high) * ncore + core, (z - high * nzl) * nx + x)

    nz = nzh * nzl

    def ring(k, n):
        return min(k, n - k)

    stage_a = sorted(((ring(i, nx) + ring(k, nz), i, k) for i in range(nx) for k in range(nz) if i or k), reverse=True)
    stage_b = sorted(((ring(k, ny), k, i) for k in range(ny) for i in range(ncore) if i or k), reverse=True)
    hops_a = [far for far, _, _ in stage_a]
    stage_a = [device(y, wrap(z + k, nz), core, wrap(x + i, nx)) for _, i, k in stage_a]
    stage_b = [device(wrap(y + k, ny), z, wrap(core + i, ncore), x) for _, k, i in stage_b]

    farther = sum(far > 5 for far in hops_a)
    partners = stage_a[:farther] + neighbours + stage_a[farther:] + stage_b
    barrier = pltpu.get_barrier_semaphore()
    for who in partners[:farther + 8]:
        pl.semaphore_signal(barrier, inc=1, device_id=who, device_id_type=MESH)

    loads = [
        [pltpu.make_async_copy(src.at[:, 128 * v:128 * v + 128], raw.at[k, v], in_sem.at[k]) for v in range(4)]
        for k, src in enumerate(inputs)
    ]
    for k in (2, 3, 0, 1, 4, 5):
        for copy in loads[k]:
            copy.start()

    for who in partners[farther + 8:]:
        pl.semaphore_signal(barrier, inc=1, device_id=who, device_id_type=MESH)

    def finish(ref, sem):
        pltpu.make_async_copy(ref, ref, sem).wait()

    shape = (24, 128)
    lane, sub = iota(shape, 1), iota(shape, 0)
    lane8, sub8 = iota((8, 128), 1), iota((8, 128), 0)

    def load(k):
        finish(raw.at[k], in_sem.at[k])
        out = []
        for t in range(4):
            parts = [raw[k, v, pl.ds(t, 24, stride=4), :] for v in range(4)]
            out += deal(parts, lane)
        return out

    def pack_cols(planes, source, base, out=None):
        for t, plane in enumerate(planes):
            moved = roll(plane, base + t - source, 1)
            out = moved if out is None else jnp.where(lane == base + t, moved, out)
        return out

    def pack_rows(planes, source, base, out=None):
        for s, plane in enumerate(planes):
            tile = plane[8 * (source // 8):8 * (source // 8) + 8]
            moved = roll(tile, base + s - source % 8, 0)
            out = moved if out is None else jnp.where(sub8 == base + s, moved, out)
        return out

    rw = load(2)
    at_end = jnp.logical_and(lane == 127, col == ncol - 1)
    for t in range(4):
        rw[4 * t + 3] = jnp.where(at_end, 0.0, rw[4 * t + 3])
    dw = load(3)
    at_end = jnp.logical_and(sub == 23, row == nrow - 1)
    for s in range(4):
        dw[12 + s] = jnp.where(at_end, 0.0, dw[12 + s])
    fx = [a * b for a, b in zip(rw, load(0))]
    fy = [a * b for a, b in zip(dw, load(1))]
    anchor = load(4)
    prior = load(5)

    def behind(planes):
        return [jnp.where(lane == 0, 0.0, roll(planes[4 * t + 3], 1, 1)) for t in range(4)]

    def above(planes):
        return [jnp.where(sub == 0, 0.0, roll(planes[12 + s], 1, 0)) for s in range(4)]

    def spread(first, planes, step):
        if step == 1:
            return [first[k // 4] if k % 4 == 0 else planes[k - 1] for k in range(16)]
        return [first[k] if k < 4 else planes[k - 4] for k in range(16)]

    lw0, fl0, uw0, fu0 = behind(rw), behind(fx), above(dw), above(fy)
    lw, fl, uw, fu = spread(lw0, rw, 1), spread(fl0, fx, 1), spread(uw0, dw, 4), spread(fu0, fy, 4)
    diag = [anchor[k] + lw[k] + rw[k] + uw[k] + dw[k] for k in range(16)]
    resid = [anchor[k] * prior[k] - fx[k] - fy[k] + fl[k] + fu[k] for k in range(16)]

    def total(planes):
        while len(planes) > 1:
            planes = [a + b for a, b in zip(planes[::2], planes[1::2])]
        return planes[0]

    c_right, c_down = total(rw[3::4]), total(dw[12:])
    c_diag = total(anchor) + total(lw0) + c_right + total(uw0) + c_down
    c_resid, c_fx, c_fy = total(resid), total(fx[3::4]), total(fy[12:])

    def side_tile(coarse, planes=None, edge=None):
        h = coarse
        if planes is not None:
            h = pack_cols(planes[3::4], 127, 120, pack_cols(planes[0::4], 0, 4, h))
        if edge is not None:
            h = pack_cols(edge[3::4], 127, 116, h)
        return h

    h0, h1 = side_tile(c_right, diag, rw), side_tile(c_down, resid, fx)
    h2 = jnp.where(lane == 119, roll(c_fx, -8, 1), c_diag)
    h3 = jnp.where(
        jnp.logical_and(lane >= 4, lane < 8), roll(c_fy, 4, 1),
        jnp.where(jnp.logical_and(lane >= 120, lane < 124), roll(c_fy, -4, 1), c_resid),
    )
    for k, h in enumerate((h0, h1, h2, h3)):
        s1h[3 * k:3 * k + 3] = h.reshape(3, 8, 128)
    s1u[0] = pack_rows(diag[:4], 0, 4, c_right[:8])
    s1u[1] = pack_rows(resid[:4], 0, 4, c_down[:8])
    s1u[2] = jnp.where(sub8 < 4, c_diag[:8], roll(c_fx[:8], 4, 0))
    s1u[3] = pack_rows([rw[3], fx[3]], 0, 4, c_resid[:8])
    s1d[0] = pack_rows(diag[12:], 23, 0, c_right[16:])
    s1d[1] = pack_rows(resid[12:], 23, 0, c_down[16:])
    s1d[2] = jnp.where(sub8 >= 4, c_diag[16:], roll(c_fx[16:], 4, 0))
    s1d[3] = pack_rows([c_fy, rw[15], fx[15]], 23, 0, c_resid[16:])
    d4 = pack_rows(fy[12:], 23, 4, pack_rows(dw[12:], 23, 0))
    s1d[4] = d4

    def pack(coarse, planes, h_ref, u_ref, d_ref):
        h_ref[...] = side_tile(coarse, planes).reshape(3, 8, 128)
        u_ref[0] = pack_rows(planes[:4], 0, 4, coarse[:8])
        d_ref[0] = pack_rows(planes[12:], 23, 0, coarse[16:])

    def exchange(h, u, d, got, nu, nd, send, recv):
        nh = h.shape[0]
        plan = [(u, 1, (up, left)), (u, 2, (up, right)), (d, 4, (down, left)), (d, 5, (down, right))]
        plan += [(u, 0, (up, col)), (d, 3, (down, col))]
        plan = [
            (src, got.at[pl.ds(2 * nh + (nu * k if k < 3 else 3 * nu + nd * (k - 3)), nu if k < 3 else nd)], who)
            for src, k, who in plan
        ]
        plan += [(h, got.at[pl.ds(0, nh)], (row, left)), (h, got.at[pl.ds(nh, nh)], (row, right))]
        for src, dst, who in plan:
            pltpu.make_async_remote_copy(src, dst, send, recv, device_id=who, device_id_type=MESH).start()

    pl.semaphore_wait(barrier, len(partners))
    exchange(s1h, s1u, s1d, got1, 4, 5, sx_sem, gx_sem.at[0])
    inner = [k for k in range(16) if k >= 4 and k % 4]

    @pl.when(row >= 0)
    def _():
        for k in range(16):
            rw_ref[k] = rw[k]
            dw_ref[k] = dw[k]
        for k in inner:
            diag_ref[k] = diag[k]
            inv_ref[k] = 1.0 / diag[k]

    def assemble(own, h, v, fill=0.0):
        side = jnp.where(lane < 64, h[0], h[1])
        ring = jnp.where(jnp.logical_or(lane < 4, lane >= 124), side, fill)
        below = jnp.where(sub8 < 4, v[0], v[3])
        corner = jnp.where(
            lane8 < 4,
            jnp.where(sub8 < 4, v[1], v[4]),
            jnp.where(lane8 >= 124, jnp.where(sub8 < 4, v[2], v[5]), fill),
        )
        ends = jnp.where(sub8 < 4, v[3], v[0])
        return quad(own, ring, below, corner), side, ends

    def quad(own, ring, below, corner):
        return jnp.concatenate(
            [jnp.concatenate([own, ring], axis=1), jnp.concatenate([below, corner], axis=1)], axis=0
        )

    finish(got1, gx_sem.at[0])
    hs = [[got1[pl.ds(12 * k + 3 * f, 3)].reshape(shape) for k in range(2)] for f in range(4)]
    vs = [[got1[24 + 4 * k + f] for k in range(3)] + [got1[36 + 5 * k + f] for k in range(3)] for f in range(4)]
    from_up, from_up_right, from_up_left = (got1[36 + 5 * k + 4] for k in range(3))

    cr, diag_side, diag_ends = assemble(c_right, hs[0], vs[0])
    cd, side, ends = assemble(c_down, hs[1], vs[1])
    cdiag, _, _ = assemble(c_diag, hs[2], vs[2], 1.0)
    ext, _, _ = assemble(c_resid, hs[3], vs[3])

    lane_x, sub_x = iota((32, 256), 1), iota((32, 256), 0)
    first_col = (lane_x & 127) == 0
    first_row = jnp.logical_or(sub_x == 0, sub_x == 24)
    cdiag = cdiag + jnp.where(first_col, roll(cr, 1, 1), 0.0) + jnp.where(first_row, roll(cd, 1, 0), 0.0)
    across = quad(
        roll(hs[2][1], 9, 1),
        roll(c_fx, 1, 1),
        roll(roll(jnp.where(sub8 < 4, vs[2][5], vs[2][2]), 4, 0), 1, 1),
        roll(roll(jnp.where(sub8 < 4, vs[2][3], vs[2][0]), 4, 0), 1, 1),
    )
    ext = ext + jnp.where(first_col, across, 0.0)
    beyond = jnp.where(lane8 < 64, vs[3][4], vs[3][5])
    near = jnp.where(lane < 64, roll(hs[3][0], -4, 1), roll(hs[3][1], 4, 1))
    across = quad(
        jnp.broadcast_to(vs[3][3][0:1], shape),
        jnp.broadcast_to(beyond[0:1], shape),
        roll(c_fy[16:], 1, 0),
        roll(near[16:], 1, 0),
    )
    in_ring = jnp.logical_or(lane_x < 132, lane_x >= 252)
    ext = ext + jnp.where(jnp.logical_and(first_row, in_ring), across, 0.0)

    to_right = jnp.logical_and(lane >= 4, lane < 8)
    to_left = jnp.logical_and(lane >= 120, lane < 124)
    top_right = jnp.logical_and(sub == 0, lane == 4)
    top_left = jnp.logical_and(sub == 0, lane == 120)
    far_right, far_left = roll(from_up_right, 4, 1), roll(from_up_left, -7, 1)
    col_up, col_down = roll(vs[3][5], 1, 1), roll(vs[3][2], 1, 1)
    up_corner = jnp.logical_and(lane8 == 0, sub8 == 0)
    down_corner = jnp.logical_and(lane8 == 0, sub8 == 4)

    def complete(at_side, at_ends, edge, row_edge, n):
        at_side = at_side + jnp.where(to_right, roll(edge, 16, 1), 0.0)
        at_side = at_side + jnp.where(top_right, jnp.broadcast_to(far_right[4 * n:4 * n + 1], shape), 0.0)
        at_side = at_side + jnp.where(top_left, jnp.broadcast_to(far_left[4 * n + 3:4 * n + 4], shape), 0.0)
        at_ends = at_ends + jnp.where(sub8 >= 4, row_edge, 0.0)
        at_ends = at_ends + jnp.where(up_corner, jnp.broadcast_to(col_up[1 + n:2 + n], (8, 128)), 0.0)
        at_ends = at_ends + jnp.where(down_corner, jnp.broadcast_to(col_down[4 + n:5 + n], (8, 128)), 0.0)
        return at_side, at_ends

    diag_side, diag_ends = complete(diag_side, diag_ends, h0, roll(d4, 4, 0), 0)
    side, ends = complete(side, ends, h1, d4, 1)
    inv_side = 1.0 / jnp.where(jnp.logical_or(to_right, to_left), diag_side, 1.0)
    inv_ends = 1.0 / diag_ends

    for t in range(4):
        more = jnp.where(lane == 0, roll(hs[0][1], -(116 + t), 1), 0.0)
        lw0[t] = lw0[t] + more
        diag[4 * t] = diag[4 * t] + more
        resid[4 * t] = resid[4 * t] + jnp.where(lane == 0, roll(hs[1][1], -(116 + t), 1), 0.0)
    for s in range(4):
        more = jnp.where(sub == 0, jnp.broadcast_to(from_up[s:s + 1], shape), 0.0)
        uw0[s] = uw0[s] + more
        diag[s] = diag[s] + more
        resid[s] = resid[s] + jnp.where(sub == 0, jnp.broadcast_to(from_up[4 + s:5 + s], shape), 0.0)
    for k in range(16):
        if k not in inner:
            diag_ref[k] = diag[k]
            inv_ref[k] = 1.0 / diag[k]
    for k in range(4):
        lw_ref[k] = lw0[k]
        uw_ref[k] = uw0[k]

    scale = OMEGA / cdiag
    a_right, a_left = scale * cr, scale * roll(cr, 1, 1)
    a_down, a_up = scale * cd, scale * roll(cd, 1, 0)

    def smooth(ext, side, ends):
        start = scale * ext
        level = start
        for turn in range(3):
            beside = a_left * roll(level, 1, 1) + a_right * roll(level, -1, 1)
            beside = beside + a_up * roll(level, 1, 0) + a_down * roll(level, -1, 0)
            level = (1.0 - OMEGA) * level + (start + beside)
        e_side, e_ends = level[:24, 128:], level[24:, :128]
        e_side = jnp.where(
            lane < 64, jnp.broadcast_to(e_side[:, 0:1], shape), jnp.broadcast_to(e_side[:, 127:128], shape)
        )
        e_ends = jnp.where(
            sub8 < 4, jnp.broadcast_to(e_ends[7:8], (8, 128)), jnp.broadcast_to(e_ends[0:1], (8, 128))
        )
        return level, inv_side * side + e_side, inv_ends * ends + e_ends

    def borders(side, ends):
        west = [jnp.where(lane == 0, roll(side, -(120 + t), 1), 0.0) for t in range(4)]
        east = [jnp.where(lane == 127, roll(side, 127 - (4 + t), 1), 0.0) for t in range(4)]
        north = [jnp.where(sub == 0, jnp.broadcast_to(ends[s:s + 1], shape), 0.0) for s in range(4)]
        south = [jnp.where(sub == 23, jnp.broadcast_to(ends[4 + s:5 + s], shape), 0.0) for s in range(4)]
        return west, east, north, south

    def operate(v, around=None):
        west = [jnp.where(lane == 0, 0.0 if around is None else around[0][t], roll(v[4 * t + 3], 1, 1)) for t in range(4)]
        east = [jnp.where(lane == 127, 0.0 if around is None else around[1][t], roll(v[4 * t], -1, 1)) for t in range(4)]
        north = [jnp.where(sub == 0, 0.0 if around is None else around[2][s], roll(v[12 + s], 1, 0)) for s in range(4)]
        south = [jnp.where(sub == 23, 0.0 if around is None else around[3][s], roll(v[s], -1, 0)) for s in range(4)]
        image = []
        for k in range(16):
            t, s = k // 4, k % 4
            beside = (lw_ref[t] * west[t]) if s == 0 else (rw_ref[k - 1] * v[k - 1])
            beside = beside + rw_ref[k] * (east[t] if s == 3 else v[k + 1])
            beside = beside + ((uw_ref[s] * north[s]) if t == 0 else (dw_ref[k - 4] * v[k - 4]))
            beside = beside + dw_ref[k] * (south[s] if t == 3 else v[k + 4])
            image.append(diag_ref[k] * v[k] - beside)
        return image

    def dot(a, b):
        return total([a[k] * b[k] for k in range(16)])

    def fold(x):
        return x[:8] + x[8:16] + x[16:]

    order = [("g", 0), ("g", 1), ("g", 2), (0, 0), (0, 1), (0, 2), (1, 1), (1, 2), (2, 2)]
    news = ext, side, ends
    coarses, images = [ext[:24, :128]], [resid]
    for j in range(2):
        if j:
            finish(got[j - 1], gx_sem.at[j])
            news = assemble(
                coarses[j], [got[j - 1][3 * k:3 * k + 3].reshape(shape) for k in range(2)], [got[j - 1][6 + k] for k in range(6)]
            )
        level, new_side, new_ends = smooth(*news)
        own = level[:24, :128]
        if j == 0:
            v = [inv_ref[k] * resid[k] + own for k in range(16)]
            side, ends = new_side, new_ends
        else:
            v = [inv_ref[k] * images[j][k] + own - u_ref[0, k] for k in range(16)]
            side, ends = new_side - side, new_ends - ends
        image = operate(v, borders(side, ends))
        images.append(image)
        coarses.append(total(image))
        pack(coarses[-1], image, sh.at[j], su.at[j], sd.at[j])
        exchange(sh.at[j], su.at[j], sd.at[j], got[j], 1, 1, sx_sem, gx_sem.at[j + 1])
        for k in range(16):
            u_ref[j, k] = v[k]
            w_ref[j, k] = image[k]

        @pl.when(row >= 0)
        def _():
            v = [u_ref[j, k] for k in range(16)]
            sums_ref[order.index(("g", j))] = fold(dot(resid, v))
            for i in range(j + 1):
                sums_ref[order.index((i, j))] = fold(dot([w_ref[i, k] for k in range(16)], v))
            if j == 1:
                last = [w_ref[1, k] for k in range(16)]
                p = [inv_ref[k] * last[k] - v[k] for k in range(16)]
                image = operate(p)
                for k in range(16):
                    u_ref[2, k] = p[k]
                sums_ref[2] = fold(dot(resid, p))
                sums_ref[5] = fold(dot([w_ref[0, k] for k in range(16)], p))
                sums_ref[7] = fold(dot(last, p))
                sums_ref[8] = fold(dot(image, p))
                coarse_ref[...] = total(image)

    finish(got[1], gx_sem.at[2])
    ext, new_side, new_ends = assemble(
        coarses[2], [got[1][3 * k:3 * k + 3].reshape(shape) for k in range(2)], [got[1][6 + k] for k in range(6)]
    )
    p_side, p_ends = inv_side * new_side - side, inv_ends * new_ends - ends
    level, new_side, new_ends = smooth(ext, new_side, new_ends)
    side, ends = new_side - side, new_ends - ends
    own = level[:24, :128]
    beside = cr * roll(level, -1, 1) + roll(cr * level, 1, 1) + cd * roll(level, -1, 0) + roll(cd * level, 1, 0)
    c_image = (cdiag * level - beside)[:24, :128]
    cross, power = [], []
    west, east, north, south = borders(p_side, p_ends)
    for q in range(4):
        for weight, beyond, k in (
            (lw_ref[q], west[q], 4 * q), (rw_ref[4 * q + 3], east[q], 4 * q + 3),
            (uw_ref[q], north[q], q), (dw_ref[12 + q], south[q], 12 + q),
        ):
            flow = weight * beyond
            cross.append(flow)
            power.append(flow * u_ref[2, k])
    p_image = coarse_ref[...] - total(cross)
    sums = {name: sums_ref[k] for k, name in enumerate(order)}
    sums["g", 2] = sums["g", 2] + fold(coarses[0] * own)
    sums[0, 2] = sums[0, 2] + fold(coarses[1] * own)
    sums[1, 2] = sums[1, 2] + fold(coarses[2] * own)
    sums[2, 2] = sums[2, 2] + fold((c_image + 2.0 * p_image) * own - total(power))

    sums_row = jnp.zeros((1, 128), F)
    lane1 = iota((1, 128), 1)
    for k, name in enumerate(order):
        x8 = sums[name]
        for shift in (64, 32, 16, 8):
            x8 = x8 + roll(x8, shift, 1)
        one = jnp.sum(x8, axis=0, keepdims=True)
        sums_row = jnp.where((lane1 >> 3) == k, one, sums_row)

    def keep(n, planes):
        for t in range(4):
            for v, value in enumerate(undeal(planes[4 * t:4 * t + 4], lane)):
                kept_ref[n, v, pl.ds(t, 24, stride=4), :] = value

    base = 0
    for stage, others in enumerate((stage_b, stage_a)):
        part[stage] = sums_row
        for k, who in enumerate(others):
            pltpu.make_async_remote_copy(
                part.at[stage], slots.at[base + k], sr_sem, gr_sem.at[stage], device_id=who, device_id_type=MESH
            ).start()

        @pl.when(row >= 0)
        def _():
            if stage == 0:
                v = [u_ref[2, k] + own for k in range(16)]
                keep(3, v)
                keep(6, operate(v, borders(side, ends)))
            else:
                keep(0, resid)
                for j in range(2):
                    keep(1 + j, [u_ref[j, k] for k in range(16)])
                    keep(4 + j, [w_ref[j, k] for k in range(16)])

        finish(slots.at[pl.ds(base, len(others))], gr_sem.at[stage])
        sums_row = total_any([sums_row] + [slots[base + k] for k in range(len(others))])
        base += len(others)

    for shift in (4, 2, 1):
        sums_row = sums_row + roll(sums_row, -shift, 1)
    value = {
        name: jnp.broadcast_to(sums_row[:, 8 * k:8 * k + 1], (1, 128)) for k, name in enumerate(order)
    }
    g0, g1, g2 = (value["g", j] for j in range(3))
    a00, a01, a02 = value[0, 0], value[0, 1], value[0, 2]
    l10, l20 = a01 / a00, a02 / a00
    d1, t12 = value[1, 1] - l10 * a01, value[1, 2] - l10 * a02
    l21 = t12 / d1
    d2 = value[2, 2] - l20 * a02 - l21 * t12
    y1 = g1 - l10 * g0
    y2 = g2 - l20 * g0 - l21 * y1
    c2 = y2 / d2
    c1 = y1 / d1 - l21 * c2
    c0 = g0 / a00 - l10 * c1 - l20 * c2
    for k, value in enumerate((c0, c1, c2)):
        c_ref[k] = jnp.broadcast_to(value, (8, 128))

    finish(landed, sx_sem)
    finish(slots, sr_sem)


def combine(kept_ref, c_ref, heights_ref, resid_ref, done, sem):
    c = [c_ref[k] for k in range(3)]
    for v in range(4):
        for i in range(0, kept_ref.shape[2], 8):
            r0, u0, u1, u2, w0, w1, w2 = (kept_ref[n, v, i:i + 8] for n in range(7))
            done[0, v, i:i + 8] = c[0] * u0 + c[1] * u1 + c[2] * u2
            done[1, v, i:i + 8] = r0 - (c[0] * w0 + c[1] * w1 + c[2] * w2)
        for n, out_ref in enumerate((heights_ref, resid_ref)):
            pltpu.make_async_copy(done.at[n, v], out_ref.at[:, 128 * v:128 * v + 128], sem).start()
    pltpu.make_async_copy(done, done, sem).wait()


def total_any(values):
    while len(values) > 1:
        rest = values[len(values) // 2 * 2:]
        values = [a + b for a, b in zip(values[::2], values[1::2])] + rest
    return values[0]


def solution(mesh, split=SPLIT):
    others = split["x"] * split["zh"] * split["zl"] + split["y"] * split["core"] - 2

    def step(*args):
        rows, cols = args[0].shape
        assert (rows, cols) == (96, 512)
        shapes = [(7, 4, rows, 128), (3, 8, 128)]
        dma = pltpu.SemaphoreType.DMA

        def vmem(*shape):
            return pltpu.VMEM(shape, F)

        args = [pltpu.with_memory_space_constraint(x, pltpu.HBM) for x in args]
        parts = pl.pallas_call(
            functools.partial(kernel, split),
            out_shape=[jax.ShapeDtypeStruct(shape, F) for shape in shapes],
            in_specs=[pl.BlockSpec(memory_space=pltpu.HBM)] * 6,
            out_specs=[pl.BlockSpec(memory_space=pltpu.VMEM)] * 2,
            scratch_shapes=[
                vmem(6, 4, rows, 128),
                vmem(16, 24, 128), vmem(16, 24, 128), vmem(16, 24, 128), vmem(16, 24, 128),
                vmem(4, 24, 128), vmem(4, 24, 128),
                vmem(3, 16, 24, 128), vmem(2, 16, 24, 128), vmem(9, 8, 128), vmem(24, 128),
                vmem(12, 8, 128), vmem(4, 8, 128), vmem(5, 8, 128),
                vmem(2, 3, 8, 128), vmem(2, 1, 8, 128), vmem(2, 1, 8, 128), vmem(75, 8, 128),
                vmem(2, 1, 128), vmem(others, 1, 128),
                dma((6,)), dma(()), dma((3,)), dma(()), dma((2,)),
            ],
            compiler_params=pltpu.CompilerParams(
                collective_id=0, has_side_effects=True, vmem_limit_bytes=12 * 2**20
            ),
        )(*args)
        return tuple(pl.pallas_call(
            combine,
            out_shape=[jax.ShapeDtypeStruct((rows, cols), F)] * 2,
            in_specs=[pl.BlockSpec(memory_space=pltpu.VMEM)] * 2,
            out_specs=[pl.BlockSpec(memory_space=pltpu.HBM)] * 2,
            scratch_shapes=[vmem(2, 4, rows, 128), dma(())],
            compiler_params=pltpu.CompilerParams(vmem_limit_bytes=12 * 2**20),
        )(*parts))

    return jax.shard_map(
        step,
        mesh=mesh,
        in_specs=(P("row", "col"),) * 6,
        out_specs=(P("row", "col"),) * 2,
        check_vma=False,
    )
```
